256 devices in a mesh: row: 8 (over z_lo, y), col: 32 (over x, z_hi, core).
Axes of the slice: x: 4, y: 4, z: 8 (z_hi: 4, z_lo: 2; z = z_hi * 2 + z_lo), core: 2. Of those that a mesh axis runs over, the one named last changes fastest.
Arguments:
- feature_map: bfloat16 [1024, 1024, 64], P('row', 'col'), may hold values from -6 to 6
- first_conv_weight: bfloat16 [3, 3, 64, 64], replicated, may hold values from -0.25 to 0.25
- first_conv_bias: float32 [64], replicated, may hold values from -3 to 3
- second_conv_weight: bfloat16 [3, 3, 64, 64], replicated, may hold values from -0.25 to 0.25
- second_conv_bias: float32 [64], replicated, may hold values from -3 to 3
- cotangent: bfloat16 [1024, 1024, 64], P('row', 'col'), may hold values from -6 to 6
Outputs:
- output: bfloat16 [1024, 1024, 64], P('row', 'col')
- grad_input: bfloat16 [1024, 1024, 64], P('row', 'col')
The draws below stay inside these ranges and needn't reach their ends.
All inputs are finite; a program needn't handle non-finite values.
Results may differ from the reference program's by a relative error of at most 0.0058.
Values may be sent and summed in bfloat16 or wider, within the bound.
A program may use at most 64 MiB of HBM per device.

```python
import jax
import jax.numpy as jnp
from jax import lax

C = 64
DILATION_STEP = 4
NB = 1024
N_ROW = 8


def level_of(stream_key, shape, cuts, smallest, top_value):
    factor_of = 1.0
    for position, parts in cuts:
        heights = jax.random.uniform(jax.random.fold_in(jax.random.fold_in(stream_key, 6), position), (parts,), jnp.float32, smallest / len(cuts), top_value / len(cuts))
        factor_of = factor_of * jnp.repeat(jnp.exp(heights), shape[position] // parts).reshape((-1,) + (1,) * (len(shape) - 1 - position))
    return factor_of


def scatter_about(stream_key, extent, spread, reach, shards=(), held_as=jnp.bfloat16):
    factor_of = level_of(stream_key, extent, shards, -0.22, 0.18) if shards else 1.0
    array = jax.random.normal(stream_key, extent, jnp.float32) * spread * factor_of
    return jnp.minimum(jnp.maximum(array, -reach), reach).astype(held_as)


def setup_inputs(seed: int = 0) -> dict:
    key_list = jax.random.split(jax.random.key(seed), 7)
    return {
        "feature_map": scatter_about(key_list[0], (NB, NB, C), 1.0, 6.0, ((0, 8), (1, 32))),
        "first_conv_weight": scatter_about(key_list[1], (3, 3, C, C), (9 * C) ** -0.5, 0.25),
        "first_conv_bias": scatter_about(key_list[2], (C,), 0.5, 3.0, (), jnp.float32),
        "second_conv_weight": scatter_about(key_list[3], (3, 3, C, C), (9 * C) ** -0.5, 0.25),
        "second_conv_bias": scatter_about(key_list[4], (C,), 0.5, 3.0, (), jnp.float32),
        "cotangent": scatter_about(key_list[5], (NB, NB, C), 1.0, 6.0, ((0, 8), (1, 32))),
    }


root_half = 0.7071067811865476
inv_root_tau = 0.3989422804014327


def gelu_value(value_array):
    return 0.5 * value_array * (1.0 + lax.erf(value_array * root_half))


def gelu_slope(value_array):
    return 0.5 * (1.0 + lax.erf(value_array * root_half)) + value_array * jnp.exp(-0.5 * value_array * value_array) * inv_root_tau


def dilated_conv(padded_input, conv_kernel):
    return lax.conv_general_dilated(padded_input[None].astype(jnp.float32), conv_kernel.astype(jnp.float32), (1, 1), "VALID", rhs_dilation=(DILATION_STEP, DILATION_STEP), dimension_numbers=("NHWC", "HWIO", "NHWC"), precision=lax.Precision.HIGHEST)[0]


def reversed_kernel(conv_kernel):
    return jnp.transpose(conv_kernel[::-1, ::-1], (0, 1, 3, 2))


def margin(input_array):
    return jnp.pad(input_array, ((DILATION_STEP, DILATION_STEP), (DILATION_STEP, DILATION_STEP), (0, 0)))


def reference(feature_map, first_conv_weight, first_conv_bias, second_conv_weight, second_conv_bias, cotangent):
    band_len = NB // N_ROW
    offsets = jnp.arange(N_ROW, dtype=jnp.int32) * band_len

    def stacked(result):
        return result.reshape(NB, NB, C)

    def row_strip(input_array, shift_amount, extra):
        return lax.dynamic_slice_in_dim(input_array, shift_amount, band_len + extra, 0)

    def mirror_band(input_array, shift_amount):
        return jnp.transpose(lax.dynamic_slice_in_dim(input_array, shift_amount, band_len, 1), (1, 0, 2))

    def make_symmetric(shift_amount):
        total_sum = row_strip(feature_map, shift_amount, 0).astype(jnp.float32) + mirror_band(feature_map, shift_amount).astype(jnp.float32)
        return total_sum.astype(jnp.bfloat16)

    symmetric = stacked(lax.map(make_symmetric, offsets))
    symmetric_padding = margin(symmetric)

    def pre_first(shift_amount):
        return dilated_conv(row_strip(symmetric_padding, shift_amount, 2 * DILATION_STEP), first_conv_weight) + first_conv_bias

    def make_hidden(shift_amount):
        return gelu_value(pre_first(shift_amount)).astype(jnp.bfloat16)

    hidden_padding = margin(stacked(lax.map(make_hidden, offsets)))

    def second_section(shift_amount):
        second_preactivation = dilated_conv(row_strip(hidden_padding, shift_amount, 2 * DILATION_STEP), second_conv_weight) + second_conv_bias
        result = (row_strip(symmetric, shift_amount, 0).astype(jnp.float32) + gelu_value(second_preactivation)).astype(jnp.bfloat16)
        grad_second = (row_strip(cotangent, shift_amount, 0).astype(jnp.float32) * gelu_slope(second_preactivation)).astype(jnp.bfloat16)
        return result, grad_second

    result_bands, second_bands = lax.map(second_section, offsets)
    output = stacked(result_bands)
    second_padding = margin(stacked(second_bands))

    def third_section(shift_amount):
        hidden_gradient = dilated_conv(row_strip(second_padding, shift_amount, 2 * DILATION_STEP), reversed_kernel(second_conv_weight))
        return (hidden_gradient * gelu_slope(pre_first(shift_amount))).astype(jnp.bfloat16)

    first_padding = margin(stacked(lax.map(third_section, offsets)))

    def fourth_section(shift_amount):
        total_sum = row_strip(cotangent, shift_amount, 0).astype(jnp.float32) + dilated_conv(row_strip(first_padding, shift_amount, 2 * DILATION_STEP), reversed_kernel(first_conv_weight))
        return total_sum.astype(jnp.bfloat16)

    grad_sym = stacked(lax.map(fourth_section, offsets))

    def fifth_section(shift_amount):
        total_sum = row_strip(grad_sym, shift_amount, 0).astype(jnp.float32) + mirror_band(grad_sym, shift_amount).astype(jnp.float32)
        return total_sum.astype(jnp.bfloat16)

    grad_input = stacked(lax.map(fifth_section, offsets))
    return output, grad_input
```

```python
import functools

import jax
import jax.numpy as jnp
from jax import lax
from jax.experimental import pallas as pl
from jax.experimental.pallas import tpu as pltpu
from jax.sharding import PartitionSpec as P

MESH = pl.DeviceIdType.MESH
STEP = 4
PHASES = STEP * STEP
F32 = jnp.float32
BF16 = jnp.bfloat16
ROOT_HALF = 0.7071067811865476
INV_ROOT_TAU = 0.3989422804014327
DIRECTIONS = [(-1, 0), (1, 0), (0, -1), (0, 1), (-1, -1), (-1, 1), (1, -1), (1, 1)]
NT = (((1,), (1,)), ((), ()))
TN = (((0,), (0,)), ((), ()))


def iota2(shape, dim):
    return lax.broadcasted_iota(jnp.int32, shape, dim)


def dot(a, b, dims=None):
    if dims is None:
        return jnp.dot(a, b, preferred_element_type=F32)
    return lax.dot_general(a, b, dims, preferred_element_type=F32)


def gelu_and_slope(v):
    half_cdf = 0.5 * (1.0 + lax.erf(v * ROOT_HALF))
    return v * half_cdf, half_cdf + v * jnp.exp(-0.5 * v * v) * INV_ROOT_TAU


def gelu_value(v):
    return 0.5 * v * (1.0 + lax.erf(v * ROOT_HALF))


def kernel(
    rows_axis,
    cols_axis,
    feature,
    w_first,
    b_first,
    w_second,
    b_second,
    cotangent,
    out_ref,
    grad_ref,
    entry,
    own,
    cot,
    sym,
    hid,
    g2,
    g1,
    gsym,
    fresh,
    slope,
    packed,
    inbox1,
    inbox2,
    halo_send,
    halo_recv,
    turn_send,
    turn_recv,
):
    C = w_first.shape[-1]
    TC, _, TR = feature.shape
    nI, nP = TR // STEP, TC // (2 * STEP)
    QB = TC // STEP
    NQ = TR // TC
    L = 2 * C
    r, c = lax.axis_index("row"), lax.axis_index("col")

    def partner(q):
        return (c // NQ, r * NQ + q)

    def is_self(q):
        return jnp.logical_and(c // NQ == r, r * NQ + q == c)

    def exists(d):
        dr, dc = d
        ok = None
        for delta, pos, size in ((dr, r, rows_axis), (dc, c, cols_axis)):
            if delta == -1:
                cond = pos > 0
            elif delta == 1:
                cond = pos < size - 1
            else:
                continue
            ok = cond if ok is None else jnp.logical_and(ok, cond)
        return ok

    for img in (sym, g2):
        img[0:2] = jnp.zeros((2, nP + 2, PHASES, L), BF16)
        img[nI + 2 : nI + 4] = jnp.zeros((2, nP + 2, PHASES, L), BF16)
        img[:, 0:1] = jnp.zeros((nI + 4, 1, PHASES, L), BF16)
        img[:, nP + 1 : nP + 2] = jnp.zeros((nI + 4, 1, PHASES, L), BF16)

    barrier = pltpu.get_barrier_semaphore()
    expected = jnp.int32(0)
    for q in range(NQ):
        other = jnp.logical_not(is_self(q))
        expected = expected + other.astype(jnp.int32)

        @pl.when(other)
        def _():
            pl.semaphore_signal(barrier, inc=1, device_id=partner(q), device_id_type=MESH)

    for d in DIRECTIONS:
        here = exists(d)
        expected = expected + here.astype(jnp.int32)

        @pl.when(here)
        def _():
            pl.semaphore_signal(
                barrier, inc=1, device_id=(r + d[0], c + d[1]), device_id_type=MESH
            )

    shape = (nI * PHASES, STEP * TR)
    at = iota2(shape, 0)
    target = ((at // STEP) % STEP) * TR + (at // PHASES) * STEP + at % STEP
    entry[...] = jnp.where(iota2(shape, 1) == target, 1.0, 0.0).astype(BF16)

    def enter(src, dst):
        for jp in range(nP):
            base = jp * 2 * STEP
            blocks = [
                jnp.concatenate([src[base + s], src[base + STEP + s]], axis=0) for s in range(STEP)
            ]
            res = dot(entry[...], jnp.concatenate(blocks, axis=1), NT)
            dst[:, jp] = res.astype(BF16).reshape(nI, PHASES, L)

    def leave(src, dst):
        for jp in range(nP):
            base = jp * 2 * STEP
            res = dot(src[:, jp].reshape(nI * PHASES, L), entry[...], TN).astype(BF16)
            for b in range(2):
                for s in range(STEP):
                    dst[base + STEP * b + s] = res[b * C : (b + 1) * C, s * TR : (s + 1) * TR]

    def turn_copy(src, inbox, k, q):
        return pltpu.make_async_remote_copy(
            src_ref=src.at[pl.ds(q * QB, QB)],
            dst_ref=inbox.at[lax.rem(c, NQ)],
            send_sem=turn_send.at[k, q],
            recv_sem=turn_recv.at[k, lax.rem(c, NQ)],
            device_id=partner(q),
            device_id_type=MESH,
        )

    def turn_start(src, inbox, k, q):
        mine = is_self(q)

        @pl.when(jnp.logical_not(mine))
        def _():
            turn_copy(src, inbox, k, q).start()

        @pl.when(mine)
        def _():
            pltpu.make_async_copy(
                src.at[pl.ds(q * QB, QB)], inbox.at[q], turn_recv.at[k, q]
            ).start()

    def turn_wait_recv(src, inbox, k, q):
        pltpu.make_async_copy(src.at[pl.ds(q * QB, QB)], inbox.at[q], turn_recv.at[k, q]).wait()

    def turn_wait_send(src, inbox, k):
        for q in range(NQ):

            @pl.when(jnp.logical_not(is_self(q)))
            def _():
                turn_copy(src, inbox, k, q).wait_send()

    def swap_matrices():
        n = PHASES * 8
        x, y = iota2((n, n), 0), iota2((n, n), 1)
        flipped = (x // PHASES) * PHASES + (x % STEP) * STEP + (x // STEP) % STEP
        phase = jnp.where(y == flipped, 1.0, 0.0).astype(BF16)
        m = 2 * L
        x, y = iota2((m, m), 0), iota2((m, m), 1)
        flipped = ((x // C) % 2) * L + (x // L) * C + x % C
        lanes = jnp.where(y == flipped, 1.0, 0.0).astype(BF16)
        return phase, lanes

    def turned(inbox, q, phase, lanes):
        got = inbox[q].reshape(nP, 2, nP, PHASES, L)
        pair = jnp.concatenate([got[:, 0], got[:, 1]], axis=-1).reshape(nP * nP * PHASES, 2 * L)
        swapped = dot(pair, lanes).astype(BF16)
        n = phase.shape[0]
        parts = [
            dot(phase, swapped[i * n : (i + 1) * n]).astype(BF16)
            for i in range(nP * nP * PHASES // n)
        ]
        return jnp.concatenate(parts, axis=0).reshape(nP, nP, PHASES, 2 * L)

    def halo_copy(img, k, n):
        dr, dc = DIRECTIONS[n]
        rows = {-1: (2, nI + 2, 2), 0: (2, 2, nI), 1: (nI, 0, 2)}[dr]
        cols = {-1: (1, nP + 1, 1), 0: (1, 1, nP), 1: (nP, 0, 1)}[dc]
        return pltpu.make_async_remote_copy(
            src_ref=img.at[pl.ds(rows[0], rows[2]), pl.ds(cols[0], cols[2])],
            dst_ref=img.at[pl.ds(rows[1], rows[2]), pl.ds(cols[1], cols[2])],
            send_sem=halo_send.at[k, n],
            recv_sem=halo_recv.at[k, n],
            device_id=(r + dr, c + dc),
            device_id_type=MESH,
        )

    def halo_start(img, k):
        for n in (2, 3, 4, 5, 6, 7, 0, 1):

            @pl.when(exists(DIRECTIONS[n]))
            def _():
                halo_copy(img, k, n).start()

    def halo_wait(img, k):
        for n, (dr, dc) in enumerate(DIRECTIONS):

            @pl.when(exists((-dr, -dc)))
            def _():
                halo_copy(img, k, n).wait_recv()

            @pl.when(exists((dr, dc)))
            def _():
                halo_copy(img, k, n).wait_send()

    def conv(src, k0, count, pairs, which):
        taps = []
        for dy in range(3):
            got = src[pl.ds(k0 + dy, count)]
            for side in range(2):
                taps.append(got[:, side : side + pairs].reshape(count * pairs * PHASES, L))
        return dot(jnp.concatenate(taps, axis=1), packed[which])

    def clear_outside(img):
        @pl.when(r == 0)
        def _():
            img[0] = jnp.zeros((nP + 1, PHASES, L), BF16)

        @pl.when(r == rows_axis - 1)
        def _():
            img[nI + 1] = jnp.zeros((nP + 1, PHASES, L), BF16)

        @pl.when(c == 0)
        def _():
            img[:, 0, :, 0:C] = jnp.zeros((nI + 2, PHASES, C), BF16)

        @pl.when(c == cols_axis - 1)
        def _():
            img[:, nP, :, C:L] = jnp.zeros((nI + 2, PHASES, C), BF16)

    enter(feature, own)
    pl.semaphore_wait(barrier, expected)
    for q in range(NQ):
        turn_start(own, inbox1, 0, q)

    enter(cotangent, cot)
    eye = jnp.where(iota2((C, C), 0) == iota2((C, C), 1), 1.0, 0.0).astype(BF16)
    nothing = jnp.zeros((C, C), BF16)
    for which, w, back in ((0, w_first, 0), (1, w_second, 0), (2, w_second, 1), (3, w_first, 1)):
        for dy in range(3):
            tap = [
                dot(eye, w[2 - dy, 2 - kx], NT).astype(BF16) if back else w[dy, kx]
                for kx in range(3)
            ]
            for a in range(4):
                left = tap[a] if a < 3 else nothing
                right = tap[a - 1] if a > 0 else nothing
                packed[which, pl.ds(dy * 4 * C + a * C, C)] = jnp.concatenate([left, right], axis=1)
    bias1 = jnp.concatenate([b_first[...], b_first[...]], axis=1)
    bias2 = jnp.concatenate([b_second[...], b_second[...]], axis=1)

    phase, lanes = swap_matrices()
    for q in range(NQ):
        turn_wait_recv(own, inbox1, 0, q)
        got = turned(inbox1, q, phase, lanes)
        for jp in range(nP):
            for b in range(2):
                i = q * QB + 2 * jp + b
                total = own[i].astype(F32) + got[:, jp, :, b * L : (b + 1) * L].astype(F32)
                sym[i + 2, 1 : nP + 1] = total.astype(BF16)

    halo_start(sym, 0)
    turn_wait_send(own, inbox1, 0)
    halo_wait(sym, 0)

    half = (nI + 2) // 2

    @pl.loop(0, 2)
    def _(t):
        k0 = t * half
        pre = conv(sym, k0, half, nP + 1, 0) + bias1
        value, rise = gelu_and_slope(pre)
        hid[pl.ds(k0, half)] = value.astype(BF16).reshape(half, nP + 1, PHASES, L)
        slope[pl.ds(k0, half)] = rise.reshape(half, nP + 1, PHASES, L)

    clear_outside(hid)

    @pl.loop(0, NQ)
    def _(t):
        k0 = t * QB
        pre = conv(hid, k0, QB, nP, 1) + bias2
        value, rise = gelu_and_slope(pre)
        size = (QB, nP, PHASES, L)
        base = sym[pl.ds(k0 + 2, QB)][:, 1 : nP + 1].astype(F32)
        fresh[pl.ds(k0, QB)] = (base + value.reshape(size)).astype(BF16)
        pull = cot[pl.ds(k0, QB)].astype(F32) * rise.reshape(size)
        g2[pl.ds(k0 + 2, QB), 1 : nP + 1] = pull.astype(BF16)

    halo_start(g2, 1)
    leave(fresh, out_ref)
    halo_wait(g2, 1)

    @pl.loop(0, 2)
    def _(t):
        k0 = t * half
        pulled = conv(g2, k0, half, nP + 1, 2).reshape(half, nP + 1, PHASES, L)
        g1[pl.ds(k0, half)] = (pulled * slope[pl.ds(k0, half)]).astype(BF16)

    clear_outside(g1)

    for q in range(NQ):
        k0 = q * QB
        total = conv(g1, k0, QB, nP, 3).reshape(QB, nP, PHASES, L)
        gsym[pl.ds(k0, QB)] = (cot[pl.ds(k0, QB)].astype(F32) + total).astype(BF16)
        turn_start(gsym, inbox2, 1, q)

    for q in range(NQ):
        turn_wait_recv(gsym, inbox2, 1, q)
        got = turned(inbox2, q, phase, lanes)
        for jp in range(nP):
            for b in range(2):
                i = q * QB + 2 * jp + b
                total = gsym[i].astype(F32) + got[:, jp, :, b * L : (b + 1) * L].astype(F32)
                fresh[i] = total.astype(BF16)
    turn_wait_send(gsym, inbox2, 1)
    leave(fresh, grad_ref)


def per_device(rows_axis, cols_axis, feature, w1, b1, w2, b2, cotangent):
    TR, TC, C = feature.shape
    nI, nP = TR // STEP, TC // (2 * STEP)
    QB, NQ, L = TC // STEP, TR // TC, 2 * C
    turned = lambda x: jnp.transpose(x, (1, 2, 0))
    image = lambda i, p: pltpu.VMEM((i, p, PHASES, L), BF16)
    vmem = pl.BlockSpec(memory_space=pltpu.VMEM)
    out = jax.ShapeDtypeStruct((TC, C, TR), BF16)
    res = pl.pallas_call(
        functools.partial(kernel, rows_axis, cols_axis),
        out_shape=(out, out),
        in_specs=[vmem] * 6,
        out_specs=(vmem, vmem),
        scratch_shapes=[
            pltpu.VMEM((nI * PHASES, STEP * TR), BF16),
            image(nI, nP),
            image(nI, nP),
            image(nI + 4, nP + 2),
            image(nI + 2, nP + 1),
            image(nI + 4, nP + 2),
            image(nI + 2, nP + 1),
            image(nI, nP),
            image(nI, nP),
            pltpu.VMEM((nI + 2, nP + 1, PHASES, L), F32),
            pltpu.VMEM((4, 12 * C, L), BF16),
            pltpu.VMEM((NQ, QB, nP, PHASES, L), BF16),
            pltpu.VMEM((NQ, QB, nP, PHASES, L), BF16),
            pltpu.SemaphoreType.DMA((2, 8)),
            pltpu.SemaphoreType.DMA((2, 8)),
            pltpu.SemaphoreType.DMA((2, NQ)),
            pltpu.SemaphoreType.DMA((2, NQ)),
        ],
        compiler_params=pltpu.CompilerParams(
            collective_id=0, has_side_effects=True, vmem_limit_bytes=60000000
        ),
    )(turned(feature), w1, b1.reshape(1, C), w2, b2.reshape(1, C), turned(cotangent))
    return tuple(jnp.transpose(x, (2, 0, 1)) for x in res)


def solution(mesh):
    specs = P("row", "col", None)
    return jax.shard_map(
        functools.partial(per_device, mesh.shape["row"], mesh.shape["col"]),
        mesh=mesh,
        in_specs=(specs, P(), P(), P(), P(), specs),
        out_specs=(specs, specs),
        check_vma=False,
    )
```

```python
import functools

import jax
import jax.numpy as jnp
from jax import lax
from jax.experimental import pallas as pl
from jax.experimental.pallas import tpu as pltpu
from jax.sharding import PartitionSpec as P

MESH = pl.DeviceIdType.MESH
STEP = 4
PHASES = STEP * STEP
F32 = jnp.float32
BF16 = jnp.bfloat16
ROOT_HALF = 0.7071067811865476
INV_ROOT_TAU = 0.3989422804014327
RELAYED = 4
SLOTS = 16
DIRECTIONS = [(-1, 0), (1, 0), (0, -1), (0, 1), (-1, -1), (-1, 1), (1, -1), (1, 1)]
NT = (((1,), (1,)), ((), ()))
TN = (((0,), (0,)), ((), ()))


def iota2(shape, dim):
    return lax.broadcasted_iota(jnp.int32, shape, dim)


def dot(a, b, dims=None):
    if dims is None:
        return jnp.dot(a, b, preferred_element_type=F32)
    return lax.dot_general(a, b, dims, preferred_element_type=F32)


def gelu_and_slope(v):
    half_cdf = 0.5 * (1.0 + lax.erf(v * ROOT_HALF))
    return v * half_cdf, half_cdf + v * jnp.exp(-0.5 * v * v) * INV_ROOT_TAU


def gelu_value(v):
    return 0.5 * v * (1.0 + lax.erf(v * ROOT_HALF))


def kernel(
    rows_axis,
    cols_axis,
    feature,
    w_first,
    b_first,
    w_second,
    b_second,
    cotangent,
    out_ref,
    grad_ref,
    entry,
    own,
    cot,
    sym,
    hid,
    g2,
    g1,
    gsym,
    fresh,
    slope,
    packed,
    inbox1,
    inbox2,
    relay1,
    relay2,
    halo_send,
    halo_recv,
    turn_send,
    turn_recv,
    relay_send,
    relay_recv,
):
    C = w_first.shape[-1]
    TC, _, TR = feature.shape
    nI, nP = TR // STEP, TC // (2 * STEP)
    QB = TC // STEP
    NQ = TR // TC
    L = 2 * C
    r, c = lax.axis_index("row"), lax.axis_index("col")

    def partner(q):
        return (c // NQ, r * NQ + q)

    def is_self(q):
        return jnp.logical_and(c // NQ == r, r * NQ + q == c)

    def same(a, b):
        return jnp.logical_and(a[0] == b[0], a[1] == b[1])

    me = (r, c)
    relaying = jnp.logical_and(r // 4 == c // 16, (c % 8) // 4 == r % 2)

    def relay_of(s, q):
        return ((s[0] // 4) * 4 + (s[1] // 4) % 4, (s[0] // 2) * 8 + s[1] % 8)

    def relay_slot(q):
        return ((c // 16) * 2 + r % 2) * 4 + q

    def slot_source(n):
        x = 2 * (n // 8) + (r % 4) // 2
        y = 2 * ((c // 8) % 2) + (n // 4) % 2
        return ((r // 4) * 4 + y, x * 8 + c % 8), n % 4

    relay_in = [((c // 16) * 4 + r % 4, (c // 8) * 8 + (r % 2) * 4 + k) for k in range(4)]
    relay_out = [relay_of(me, 0)]
    sources = [slot_source(n)[0] for n in range(0, SLOTS, 4)]
    targets = 16

    def exists(d):
        dr, dc = d
        ok = None
        for delta, pos, size in ((dr, r, rows_axis), (dc, c, cols_axis)):
            if delta == -1:
                cond = pos > 0
            elif delta == 1:
                cond = pos < size - 1
            else:
                continue
            ok = cond if ok is None else jnp.logical_and(ok, cond)
        return ok

    for img in (sym, g2):
        img[0:2] = jnp.zeros((2, nP + 2, PHASES, L), BF16)
        img[nI + 2 : nI + 4] = jnp.zeros((2, nP + 2, PHASES, L), BF16)
        img[:, 0:1] = jnp.zeros((nI + 4, 1, PHASES, L), BF16)
        img[:, nP + 1 : nP + 2] = jnp.zeros((nI + 4, 1, PHASES, L), BF16)

    barrier = pltpu.get_barrier_semaphore()
    expected = jnp.int32(0)
    for q in range(NQ):
        other = jnp.logical_not(is_self(q))
        expected = expected + other.astype(jnp.int32)

        @pl.when(other)
        def _():
            pl.semaphore_signal(barrier, inc=1, device_id=partner(q), device_id_type=MESH)

    def greet(other):
        @pl.when(jnp.logical_not(same(other, me)))
        def _():
            pl.semaphore_signal(barrier, inc=1, device_id=other, device_id_type=MESH)

    for other in relay_in:
        greet(other)
    for other in relay_out:
        expected = expected + jnp.logical_not(same(other, me)).astype(jnp.int32)

    @pl.when(relaying)
    def _():
        for other in sources:
            greet(other)

    greeted = jnp.int32(targets)
    for other in relay_in:
        greeted = greeted - same(other, me).astype(jnp.int32)
    expected = expected + jnp.where(relaying, greeted, 0)

    for d in DIRECTIONS:
        here = exists(d)
        expected = expected + here.astype(jnp.int32)

        @pl.when(here)
        def _():
            pl.semaphore_signal(
                barrier, inc=1, device_id=(r + d[0], c + d[1]), device_id_type=MESH
            )

    shape = (nI * PHASES, STEP * TR)
    at = iota2(shape, 0)
    target = ((at // STEP) % STEP) * TR + (at // PHASES) * STEP + at % STEP
    entry[...] = jnp.where(iota2(shape, 1) == target, 1.0, 0.0).astype(BF16)

    def enter(src, dst):
        for jp in range(nP):
            base = jp * 2 * STEP
            blocks = [
                jnp.concatenate([src[base + s], src[base + STEP + s]], axis=0) for s in range(STEP)
            ]
            res = dot(entry[...], jnp.concatenate(blocks, axis=1), NT)
            dst[:, jp] = res.astype(BF16).reshape(nI, PHASES, L)

    def leave(src, dst):
        for jp in range(nP):
            base = jp * 2 * STEP
            res = dot(src[:, jp].reshape(nI * PHASES, L), entry[...], TN).astype(BF16)
            for b in range(2):
                for s in range(STEP):
                    dst[base + STEP * b + s] = res[b * C : (b + 1) * C, s * TR : (s + 1) * TR]

    def by_relay(s, q):
        w = relay_of(s, q)
        t = (s[1] // NQ, s[0] * NQ + q)
        return jnp.logical_not(jnp.logical_or(same(w, s), same(w, t)))

    def part_rows(part):
        return pl.ds(0, RELAYED) if part else pl.ds(RELAYED, QB - RELAYED)

    def block(src, q, part):
        start, size = (0, RELAYED) if part else (RELAYED, QB - RELAYED)
        return src.at[pl.ds(q * QB + start, size)]

    def direct_copy(src, inbox, k, q, part):
        slot = lax.rem(c, NQ)
        return pltpu.make_async_remote_copy(
            src_ref=block(src, q, part),
            dst_ref=inbox.at[slot, part_rows(part)],
            send_sem=turn_send.at[k, q, part],
            recv_sem=turn_recv.at[k, slot, part],
            device_id=partner(q),
            device_id_type=MESH,
        )

    def first_copy(src, relay, k, q):
        return pltpu.make_async_remote_copy(
            src_ref=block(src, q, 1),
            dst_ref=relay.at[relay_slot(q)],
            send_sem=turn_send.at[k, q, 1],
            recv_sem=relay_recv.at[k, relay_slot(q)],
            device_id=relay_of(me, q),
            device_id_type=MESH,
        )

    def onward_copy(inbox, relay, k, n):
        s, q = slot_source(n)
        slot = lax.rem(s[1], NQ)
        return pltpu.make_async_remote_copy(
            src_ref=relay.at[n],
            dst_ref=inbox.at[slot, part_rows(1)],
            send_sem=relay_send.at[k, n],
            recv_sem=turn_recv.at[k, slot, 1],
            device_id=(s[1] // NQ, s[0] * NQ + q),
            device_id_type=MESH,
        )

    def local_copy(src, inbox, k, q, part):
        return pltpu.make_async_copy(
            block(src, q, part), inbox.at[q, part_rows(part)], turn_recv.at[k, q, part]
        )

    def own_relayed(q):
        return jnp.logical_and(jnp.logical_not(is_self(q)), by_relay(me, q))

    def own_direct(q):
        return jnp.logical_and(jnp.logical_not(is_self(q)), jnp.logical_not(by_relay(me, q)))

    def turn_start(src, inbox, relay, k, q):
        @pl.when(own_relayed(q))
        def _():
            first_copy(src, relay, k, q).start()

        @pl.when(own_direct(q))
        def _():
            direct_copy(src, inbox, k, q, 1).start()

        @pl.when(jnp.logical_not(is_self(q)))
        def _():
            direct_copy(src, inbox, k, q, 0).start()

        @pl.when(is_self(q))
        def _():
            for part in range(2):
                local_copy(src, inbox, k, q, part).start()

    def slot_used(n):
        s, q = slot_source(n)
        t = (s[1] // NQ, s[0] * NQ + q)
        return jnp.logical_and(jnp.logical_not(same(s, t)), by_relay(s, q))

    def turn_relay(inbox, relay, k):
        @pl.when(relaying)
        def _():
            @pl.loop(0, SLOTS)
            def _(n):
                @pl.when(slot_used(n))
                def _():
                    copy = onward_copy(inbox, relay, k, n)
                    pltpu.make_async_copy(relay.at[n], relay.at[n], relay_recv.at[k, n]).wait()
                    copy.start()

    def turn_wait_recv(src, inbox, k, q):
        for part in range(2):
            local_copy(src, inbox, k, q, part).wait()

    def turn_wait_send(src, inbox, relay, k):
        for q in range(NQ):

            @pl.when(own_relayed(q))
            def _():
                first_copy(src, relay, k, q).wait_send()

            @pl.when(own_direct(q))
            def _():
                direct_copy(src, inbox, k, q, 1).wait_send()

            @pl.when(jnp.logical_not(is_self(q)))
            def _():
                direct_copy(src, inbox, k, q, 0).wait_send()

        @pl.when(relaying)
        def _():
            @pl.loop(0, SLOTS)
            def _(n):
                @pl.when(slot_used(n))
                def _():
                    onward_copy(inbox, relay, k, n).wait_send()

    def swap_matrices():
        n = PHASES * 8
        x, y = iota2((n, n), 0), iota2((n, n), 1)
        flipped = (x // PHASES) * PHASES + (x % STEP) * STEP + (x // STEP) % STEP
        phase = jnp.where(y == flipped, 1.0, 0.0).astype(BF16)
        m = 2 * L
        x, y = iota2((m, m), 0), iota2((m, m), 1)
        flipped = ((x // C) % 2) * L + (x // L) * C + x % C
        lanes = jnp.where(y == flipped, 1.0, 0.0).astype(BF16)
        return phase, lanes

    def turned(inbox, q, phase, lanes):
        got = inbox[q].reshape(nP, 2, nP, PHASES, L)
        pair = jnp.concatenate([got[:, 0], got[:, 1]], axis=-1).reshape(nP * nP * PHASES, 2 * L)
        swapped = dot(pair, lanes).astype(BF16)
        n = phase.shape[0]
        parts = [
            dot(phase, swapped[i * n : (i + 1) * n]).astype(BF16)
            for i in range(nP * nP * PHASES // n)
        ]
        return jnp.concatenate(parts, axis=0).reshape(nP, nP, PHASES, 2 * L)

    def halo_copy(img, k, n):
        dr, dc = DIRECTIONS[n]
        rows = {-1: (2, nI + 2, 2), 0: (2, 2, nI), 1: (nI, 0, 2)}[dr]
        cols = {-1: (1, nP + 1, 1), 0: (1, 1, nP), 1: (nP, 0, 1)}[dc]
        return pltpu.make_async_remote_copy(
            src_ref=img.at[pl.ds(rows[0], rows[2]), pl.ds(cols[0], cols[2])],
            dst_ref=img.at[pl.ds(rows[1], rows[2]), pl.ds(cols[1], cols[2])],
            send_sem=halo_send.at[k, n],
            recv_sem=halo_recv.at[k, n],
            device_id=(r + dr, c + dc),
            device_id_type=MESH,
        )

    def halo_start(img, k):
        for n in (2, 3, 4, 5, 6, 7, 0, 1):

            @pl.when(exists(DIRECTIONS[n]))
            def _():
                halo_copy(img, k, n).start()

    def halo_wait(img, k):
        for n, (dr, dc) in enumerate(DIRECTIONS):

            @pl.when(exists((-dr, -dc)))
            def _():
                halo_copy(img, k, n).wait_recv()

            @pl.when(exists((dr, dc)))
            def _():
                halo_copy(img, k, n).wait_send()

    def conv(src, k0, count, pairs, which):
        taps = []
        for dy in range(3):
            got = src[pl.ds(k0 + dy, count)]
            for side in range(2):
                taps.append(got[:, side : side + pairs].reshape(count * pairs * PHASES, L))
        return dot(jnp.concatenate(taps, axis=1), packed[which])

    def clear_outside(img):
        @pl.when(r == 0)
        def _():
            img[0] = jnp.zeros((nP + 1, PHASES, L), BF16)

        @pl.when(r == rows_axis - 1)
        def _():
            img[nI + 1] = jnp.zeros((nP + 1, PHASES, L), BF16)

        @pl.when(c == 0)
        def _():
            img[:, 0, :, 0:C] = jnp.zeros((nI + 2, PHASES, C), BF16)

        @pl.when(c == cols_axis - 1)
        def _():
            img[:, nP, :, C:L] = jnp.zeros((nI + 2, PHASES, C), BF16)

    enter(feature, own)
    pl.semaphore_wait(barrier, expected)
    for q in range(NQ):
        turn_start(own, inbox1, relay1, 0, q)
    turn_relay(inbox1, relay1, 0)

    enter(cotangent, cot)
    eye = jnp.where(iota2((C, C), 0) == iota2((C, C), 1), 1.0, 0.0).astype(BF16)
    nothing = jnp.zeros((C, C), BF16)
    for which, w, back in ((0, w_first, 0), (1, w_second, 0), (2, w_second, 1), (3, w_first, 1)):
        for dy in range(3):
            tap = [
                dot(eye, w[2 - dy, 2 - kx], NT).astype(BF16) if back else w[dy, kx]
                for kx in range(3)
            ]
            for a in range(4):
                left = tap[a] if a < 3 else nothing
                right = tap[a - 1] if a > 0 else nothing
                packed[which, pl.ds(dy * 4 * C + a * C, C)] = jnp.concatenate([left, right], axis=1)
    bias1 = jnp.concatenate([b_first[...], b_first[...]], axis=1)
    bias2 = jnp.concatenate([b_second[...], b_second[...]], axis=1)

    phase, lanes = swap_matrices()
    for q in range(NQ):
        turn_wait_recv(own, inbox1, 0, q)
        got = turned(inbox1, q, phase, lanes)
        for jp in range(nP):
            for b in range(2):
                i = q * QB + 2 * jp + b
                total = own[i].astype(F32) + got[:, jp, :, b * L : (b + 1) * L].astype(F32)
                sym[i + 2, 1 : nP + 1] = total.astype(BF16)

    halo_start(sym, 0)
    turn_wait_send(own, inbox1, relay1, 0)
    halo_wait(sym, 0)

    half = (nI + 2) // 2

    @pl.loop(0, 2)
    def _(t):
        k0 = t * half
        pre = conv(sym, k0, half, nP + 1, 0) + bias1
        value, rise = gelu_and_slope(pre)
        hid[pl.ds(k0, half)] = value.astype(BF16).reshape(half, nP + 1, PHASES, L)
        slope[pl.ds(k0, half)] = rise.reshape(half, nP + 1, PHASES, L)

    clear_outside(hid)

    @pl.loop(0, NQ)
    def _(t):
        k0 = t * QB
        pre = conv(hid, k0, QB, nP, 1) + bias2
        value, rise = gelu_and_slope(pre)
        size = (QB, nP, PHASES, L)
        base = sym[pl.ds(k0 + 2, QB)][:, 1 : nP + 1].astype(F32)
        fresh[pl.ds(k0, QB)] = (base + value.reshape(size)).astype(BF16)
        pull = cot[pl.ds(k0, QB)].astype(F32) * rise.reshape(size)
        g2[pl.ds(k0 + 2, QB), 1 : nP + 1] = pull.astype(BF16)

    halo_start(g2, 1)
    leave(fresh, out_ref)
    halo_wait(g2, 1)

    @pl.loop(0, 2)
    def _(t):
        k0 = t * half
        pulled = conv(g2, k0, half, nP + 1, 2).reshape(half, nP + 1, PHASES, L)
        g1[pl.ds(k0, half)] = (pulled * slope[pl.ds(k0, half)]).astype(BF16)

    clear_outside(g1)

    for q in range(NQ):
        k0 = q * QB
        total = conv(g1, k0, QB, nP, 3).reshape(QB, nP, PHASES, L)
        gsym[pl.ds(k0, QB)] = (cot[pl.ds(k0, QB)].astype(F32) + total).astype(BF16)
        turn_start(gsym, inbox2, relay2, 1, q)
    turn_relay(inbox2, relay2, 1)

    for q in range(NQ):
        turn_wait_recv(gsym, inbox2, 1, q)
        got = turned(inbox2, q, phase, lanes)
        for jp in range(nP):
            for b in range(2):
                i = q * QB + 2 * jp + b
                total = gsym[i].astype(F32) + got[:, jp, :, b * L : (b + 1) * L].astype(F32)
                fresh[i] = total.astype(BF16)
    turn_wait_send(gsym, inbox2, relay2, 1)
    leave(fresh, grad_ref)


def per_device(rows_axis, cols_axis, feature, w1, b1, w2, b2, cotangent):
    TR, TC, C = feature.shape
    nI, nP = TR // STEP, TC // (2 * STEP)
    QB, NQ, L = TC // STEP, TR // TC, 2 * C
    turned = lambda x: jnp.transpose(x, (1, 2, 0))
    image = lambda i, p: pltpu.VMEM((i, p, PHASES, L), BF16)
    vmem = pl.BlockSpec(memory_space=pltpu.VMEM)
    out = jax.ShapeDtypeStruct((TC, C, TR), BF16)
    res = pl.pallas_call(
        functools.partial(kernel, rows_axis, cols_axis),
        out_shape=(out, out),
        in_specs=[vmem] * 6,
        out_specs=(vmem, vmem),
        scratch_shapes=[
            pltpu.VMEM((nI * PHASES, STEP * TR), BF16),
            image(nI, nP),
            image(nI, nP),
            image(nI + 4, nP + 2),
            image(nI + 2, nP + 1),
            image(nI + 4, nP + 2),
            image(nI + 2, nP + 1),
            image(nI, nP),
            image(nI, nP),
            pltpu.VMEM((nI + 2, nP + 1, PHASES, L), F32),
            pltpu.VMEM((4, 12 * C, L), BF16),
            pltpu.VMEM((NQ, QB, nP, PHASES, L), BF16),
            pltpu.VMEM((NQ, QB, nP, PHASES, L), BF16),
            pltpu.VMEM((SLOTS, RELAYED, nP, PHASES, L), BF16),
            pltpu.VMEM((SLOTS, RELAYED, nP, PHASES, L), BF16),
            pltpu.SemaphoreType.DMA((2, 8)),
            pltpu.SemaphoreType.DMA((2, 8)),
            pltpu.SemaphoreType.DMA((2, NQ, 2)),
            pltpu.SemaphoreType.DMA((2, NQ, 2)),
            pltpu.SemaphoreType.DMA((2, SLOTS)),
            pltpu.SemaphoreType.DMA((2, SLOTS)),
        ],
        compiler_params=pltpu.CompilerParams(
            collective_id=0, has_side_effects=True, vmem_limit_bytes=60000000
        ),
    )(turned(feature), w1, b1.reshape(1, C), w2, b2.reshape(1, C), turned(cotangent))
    return tuple(jnp.transpose(x, (2, 0, 1)) for x in res)


def solution(mesh):
    specs = P("row", "col", None)
    return jax.shard_map(
        functools.partial(per_device, mesh.shape["row"], mesh.shape["col"]),
        mesh=mesh,
        in_specs=(specs, P(), P(), P(), P(), specs),
        out_specs=(specs, specs),
        check_vma=False,
    )
```

```python
import functools

import jax
import jax.numpy as jnp
from jax import lax
from jax.experimental import pallas as pl
from jax.experimental.pallas import tpu as pltpu
from jax.sharding import PartitionSpec as P

MESH = pl.DeviceIdType.MESH
STEP = 4
PHASES = STEP * STEP
F32 = jnp.float32
BF16 = jnp.bfloat16
ROOT_HALF = 0.7071067811865476
INV_ROOT_TAU = 0.3989422804014327
SLOTS = 16
ROUTES = ((1224305661, 568855674),)
DIRECTIONS = [(-1, 0), (1, 0), (0, -1), (0, 1), (-1, -1), (-1, 1), (1, -1), (1, 1)]
NT = (((1,), (1,)), ((), ()))
TN = (((0,), (0,)), ((), ()))


def iota2(shape, dim):
    return lax.broadcasted_iota(jnp.int32, shape, dim)


def dot(a, b, dims=None):
    if dims is None:
        return jnp.dot(a, b, preferred_element_type=F32)
    return lax.dot_general(a, b, dims, preferred_element_type=F32)


def gelu_and_slope(v):
    half_cdf = 0.5 * (1.0 + lax.erf(v * ROOT_HALF))
    return v * half_cdf, half_cdf + v * jnp.exp(-0.5 * v * v) * INV_ROOT_TAU


def gelu_value(v):
    return 0.5 * v * (1.0 + lax.erf(v * ROOT_HALF))


def kernel(
    rows_axis,
    cols_axis,
    feature,
    w_first,
    b_first,
    w_second,
    b_second,
    cotangent,
    out_ref,
    grad_ref,
    entry,
    own,
    cot,
    sym,
    hid,
    g2,
    g1,
    gsym,
    fresh,
    slope,
    packed,
    inbox1,
    inbox2,
    relay1,
    relay2,
    halo_send,
    halo_recv,
    turn_send,
    turn_recv,
    relay_send,
    relay_recv,
):
    C = w_first.shape[-1]
    TC, _, TR = feature.shape
    nI, nP = TR // STEP, TC // (2 * STEP)
    QB = TC // STEP
    NQ = TR // TC
    L = 2 * C
    r, c = lax.axis_index("row"), lax.axis_index("col")

    def partner(q):
        return (c // NQ, r * NQ + q)

    def is_self(q):
        return jnp.logical_and(c // NQ == r, r * NQ + q == c)

    def same(a, b):
        return jnp.logical_and(a[0] == b[0], a[1] == b[1])

    me = (r, c)

    def via_xy(s, q):
        return ((s[0] // 4) * 4 + (s[1] // 4) % 4, (s[0] // 2) * 8 + s[1] % 8)

    def via_xy_slot(q):
        return ((c // 16) * 2 + r % 2) * 4 + q

    def via_xy_source(n):
        x = 2 * (n // 8) + (r % 4) // 2
        y = 2 * ((c // 8) % 2) + (n // 4) % 2
        return ((r // 4) * 4 + y, x * 8 + c % 8), n % 4

    kinds = [
        (
            via_xy,
            via_xy_slot,
            via_xy_source,
            jnp.logical_and(r // 4 == c // 16, (c % 8) // 4 == r % 2),
            [((c // 16) * 4 + r % 4, (c // 8) * 8 + (r % 2) * 4 + k) for k in range(4)],
            [via_xy_source(n)[0] for n in range(0, SLOTS, 4)],
            [via_xy(me, 0)],
            16,
            lambda m: ((m % 4) * 4 + m // 8, (m // 4) % 2),
        ),
    ]

    def taken(kind, part, s, q):
        x1, x0, y1, y0 = s[1] // 16, (s[1] // 8) % 2, (s[0] % 4) // 2, s[0] % 2
        z2, z1, z0, q1 = (s[1] % 8) // 4, (s[1] // 2) % 2, s[0] // 4, q // 2
        differ = lambda a, b: (a + b) % 2
        at = y0 + 2 * z2 + 4 * differ(x1, z0) + 8 * differ(x0, y1) + 16 * differ(z1, q1)
        words = [jnp.int32(word) for word in ROUTES[kind]]
        word = words[part] if isinstance(part, int) else jnp.where(part == 0, *words)
        w = kinds[kind][0](s, q)
        target = (s[1] // NQ, s[0] * NQ + q)
        aside = jnp.logical_not(jnp.logical_or(same(w, s), same(w, target)))
        return jnp.logical_and(aside, lax.shift_right_logical(word, at) % 2 == 1)

    def exists(d):
        dr, dc = d
        ok = None
        for delta, pos, size in ((dr, r, rows_axis), (dc, c, cols_axis)):
            if delta == -1:
                cond = pos > 0
            elif delta == 1:
                cond = pos < size - 1
            else:
                continue
            ok = cond if ok is None else jnp.logical_and(ok, cond)
        return ok

    for img in (sym, g2):
        img[0:2] = jnp.zeros((2, nP + 2, PHASES, L), BF16)
        img[nI + 2 : nI + 4] = jnp.zeros((2, nP + 2, PHASES, L), BF16)
        img[:, 0:1] = jnp.zeros((nI + 4, 1, PHASES, L), BF16)
        img[:, nP + 1 : nP + 2] = jnp.zeros((nI + 4, 1, PHASES, L), BF16)

    barrier = pltpu.get_barrier_semaphore()
    expected = jnp.int32(0)
    for q in range(NQ):
        other = jnp.logical_not(is_self(q))
        expected = expected + other.astype(jnp.int32)

        @pl.when(other)
        def _():
            pl.semaphore_signal(barrier, inc=1, device_id=partner(q), device_id_type=MESH)

    def greet(other):
        @pl.when(jnp.logical_not(same(other, me)))
        def _():
            pl.semaphore_signal(barrier, inc=1, device_id=other, device_id_type=MESH)

    for _, _, _, relaying, relays, sources, firsts, targets, _ in kinds:
        greeted = jnp.int32(targets)
        for other in relays:
            greet(other)
            greeted = greeted - same(other, me).astype(jnp.int32)
        for other in firsts:
            expected = expected + jnp.logical_not(same(other, me)).astype(jnp.int32)
        expected = expected + jnp.where(relaying, greeted, 0)

        @pl.when(relaying)
        def _():
            for other in sources:
                greet(other)

    for d in DIRECTIONS:
        here = exists(d)
        expected = expected + here.astype(jnp.int32)

        @pl.when(here)
        def _():
            pl.semaphore_signal(
                barrier, inc=1, device_id=(r + d[0], c + d[1]), device_id_type=MESH
            )

    shape = (nI * PHASES, STEP * TR)
    at = iota2(shape, 0)
    target = ((at // STEP) % STEP) * TR + (at // PHASES) * STEP + at % STEP
    entry[...] = jnp.where(iota2(shape, 1) == target, 1.0, 0.0).astype(BF16)

    def enter(src, dst):
        for jp in range(nP):
            base = jp * 2 * STEP
            blocks = [
                jnp.concatenate([src[base + s], src[base + STEP + s]], axis=0) for s in range(STEP)
            ]
            res = dot(entry[...], jnp.concatenate(blocks, axis=1), NT)
            dst[:, jp] = res.astype(BF16).reshape(nI, PHASES, L)

    def leave(src, dst):
        for jp in range(nP):
            base = jp * 2 * STEP
            res = dot(src[:, jp].reshape(nI * PHASES, L), entry[...], TN).astype(BF16)
            for b in range(2):
                for s in range(STEP):
                    dst[base + STEP * b + s] = res[b * C : (b + 1) * C, s * TR : (s + 1) * TR]

    half_rows = QB // 2

    def part_rows(part):
        return pl.ds(part * half_rows, half_rows)

    def block(src, q, part):
        return src.at[pl.ds(q * QB + part * half_rows, half_rows)]

    def direct_copy(src, inbox, k, q, part):
        slot = lax.rem(c, NQ)
        return pltpu.make_async_remote_copy(
            src_ref=block(src, q, part),
            dst_ref=inbox.at[slot, part_rows(part)],
            send_sem=turn_send.at[k, q, part],
            recv_sem=turn_recv.at[k, slot, part],
            device_id=partner(q),
            device_id_type=MESH,
        )

    def first_copy(src, relay, k, kind, q, part):
        slot = kinds[kind][1](q)
        return pltpu.make_async_remote_copy(
            src_ref=block(src, q, part),
            dst_ref=relay.at[kind, slot, part],
            send_sem=turn_send.at[k, q, part],
            recv_sem=relay_recv.at[k, kind, slot, part],
            device_id=kinds[kind][0](me, q),
            device_id_type=MESH,
        )

    def onward_copy(inbox, relay, k, kind, n, part):
        s, q = kinds[kind][2](n)
        slot = lax.rem(s[1], NQ)
        return pltpu.make_async_remote_copy(
            src_ref=relay.at[kind, n, part],
            dst_ref=inbox.at[slot, part_rows(part)],
            send_sem=relay_send.at[k, kind, n, part],
            recv_sem=turn_recv.at[k, slot, part],
            device_id=(s[1] // NQ, s[0] * NQ + q),
            device_id_type=MESH,
        )

    def local_copy(src, inbox, k, q, part):
        return pltpu.make_async_copy(
            block(src, q, part), inbox.at[q, part_rows(part)], turn_recv.at[k, q, part]
        )

    def way(q, part):
        by = [taken(kind, part, me, q) for kind in range(len(kinds))]
        straight = jnp.logical_not(is_self(q))
        for one in by:
            straight = jnp.logical_and(straight, jnp.logical_not(one))
        return by, straight

    ways = {(q, part): way(q, part) for q in range(NQ) for part in range(2)}

    def turn_start(src, inbox, relay, k, qs):
        for q in qs:
            for part in range(2):
                for kind, one in enumerate(ways[q, part][0]):

                    @pl.when(one)
                    def _():
                        first_copy(src, relay, k, kind, q, part).start()

        for q in qs:
            for part in range(2):

                @pl.when(ways[q, part][1])
                def _():
                    direct_copy(src, inbox, k, q, part).start()

            @pl.when(is_self(q))
            def _():
                for part in range(2):
                    local_copy(src, inbox, k, q, part).start()

    def slots_do(act):
        for kind, entry_of in enumerate(kinds):

            @pl.when(entry_of[3])
            def _():
                @pl.loop(0, 2 * SLOTS)
                def _(m):
                    n, part = entry_of[-1](m)
                    s, q = entry_of[2](n)

                    @pl.when(taken(kind, part, s, q))
                    def _():
                        act(kind, n, part)

    def turn_relay(inbox, relay, k):
        def act(kind, n, part):
            at = relay.at[kind, n, part]
            pltpu.make_async_copy(at, at, relay_recv.at[k, kind, n, part]).wait()
            onward_copy(inbox, relay, k, kind, n, part).start()

        slots_do(act)

    def turn_wait_recv(src, inbox, k, q):
        for part in range(2):
            local_copy(src, inbox, k, q, part).wait()

    def turn_wait_send(src, inbox, relay, k):
        for q in range(NQ):
            for part in range(2):

                @pl.when(jnp.logical_not(is_self(q)))
                def _():
                    direct_copy(src, inbox, k, q, part).wait_send()

        def act(kind, n, part):
            onward_copy(inbox, relay, k, kind, n, part).wait_send()

        slots_do(act)

    def swap_matrices():
        n = PHASES * 8
        x, y = iota2((n, n), 0), iota2((n, n), 1)
        flipped = (x // PHASES) * PHASES + (x % STEP) * STEP + (x // STEP) % STEP
        phase = jnp.where(y == flipped, 1.0, 0.0).astype(BF16)
        m = 2 * L
        x, y = iota2((m, m), 0), iota2((m, m), 1)
        flipped = ((x // C) % 2) * L + (x // L) * C + x % C
        lanes = jnp.where(y == flipped, 1.0, 0.0).astype(BF16)
        return phase, lanes

    def turned(inbox, q, phase, lanes):
        got = inbox[q].reshape(nP, 2, nP, PHASES, L)
        pair = jnp.concatenate([got[:, 0], got[:, 1]], axis=-1).reshape(nP * nP * PHASES, 2 * L)
        swapped = dot(pair, lanes).astype(BF16)
        n = phase.shape[0]
        parts = [
            dot(phase, swapped[i * n : (i + 1) * n]).astype(BF16)
            for i in range(nP * nP * PHASES // n)
        ]
        return jnp.concatenate(parts, axis=0).reshape(nP, nP, PHASES, 2 * L)

    def halo_copy(img, k, n):
        dr, dc = DIRECTIONS[n]
        rows = {-1: (2, nI + 2, 2), 0: (2, 2, nI), 1: (nI, 0, 2)}[dr]
        cols = {-1: (1, nP + 1, 1), 0: (1, 1, nP), 1: (nP, 0, 1)}[dc]
        return pltpu.make_async_remote_copy(
            src_ref=img.at[pl.ds(rows[0], rows[2]), pl.ds(cols[0], cols[2])],
            dst_ref=img.at[pl.ds(rows[1], rows[2]), pl.ds(cols[1], cols[2])],
            send_sem=halo_send.at[k, n],
            recv_sem=halo_recv.at[k, n],
            device_id=(r + dr, c + dc),
            device_id_type=MESH,
        )

    def halo_start(img, k):
        for n in (2, 3, 4, 5, 6, 7, 0, 1):

            @pl.when(exists(DIRECTIONS[n]))
            def _():
                halo_copy(img, k, n).start()

    def halo_wait(img, k):
        for n, (dr, dc) in enumerate(DIRECTIONS):

            @pl.when(exists((-dr, -dc)))
            def _():
                halo_copy(img, k, n).wait_recv()

            @pl.when(exists((dr, dc)))
            def _():
                halo_copy(img, k, n).wait_send()

    def conv(src, k0, count, pairs, which):
        taps = []
        for dy in range(3):
            got = src[pl.ds(k0 + dy, count)]
            for side in range(2):
                taps.append(got[:, side : side + pairs].reshape(count * pairs * PHASES, L))
        return dot(jnp.concatenate(taps, axis=1), packed[which])

    def clear_outside(img):
        @pl.when(r == 0)
        def _():
            img[0] = jnp.zeros((nP + 1, PHASES, L), BF16)

        @pl.when(r == rows_axis - 1)
        def _():
            img[nI + 1] = jnp.zeros((nP + 1, PHASES, L), BF16)

        @pl.when(c == 0)
        def _():
            img[:, 0, :, 0:C] = jnp.zeros((nI + 2, PHASES, C), BF16)

        @pl.when(c == cols_axis - 1)
        def _():
            img[:, nP, :, C:L] = jnp.zeros((nI + 2, PHASES, C), BF16)

    enter(feature, own)
    pl.semaphore_wait(barrier, expected)
    turn_start(own, inbox1, relay1, 0, range(NQ))
    turn_relay(inbox1, relay1, 0)

    enter(cotangent, cot)
    eye = jnp.where(iota2((C, C), 0) == iota2((C, C), 1), 1.0, 0.0).astype(BF16)
    nothing = jnp.zeros((C, C), BF16)
    for which, w, back in ((0, w_first, 0), (1, w_second, 0), (2, w_second, 1), (3, w_first, 1)):
        for dy in range(3):
            tap = [
                dot(eye, w[2 - dy, 2 - kx], NT).astype(BF16) if back else w[dy, kx]
                for kx in range(3)
            ]
            for a in range(4):
                left = tap[a] if a < 3 else nothing
                right = tap[a - 1] if a > 0 else nothing
                packed[which, pl.ds(dy * 4 * C + a * C, C)] = jnp.concatenate([left, right], axis=1)
    bias1 = jnp.concatenate([b_first[...], b_first[...]], axis=1)
    bias2 = jnp.concatenate([b_second[...], b_second[...]], axis=1)

    phase, lanes = swap_matrices()
    for q in range(NQ):
        turn_wait_recv(own, inbox1, 0, q)
        got = turned(inbox1, q, phase, lanes)
        for jp in range(nP):
            for b in range(2):
                i = q * QB + 2 * jp + b
                total = own[i].astype(F32) + got[:, jp, :, b * L : (b + 1) * L].astype(F32)
                sym[i + 2, 1 : nP + 1] = total.astype(BF16)

    halo_start(sym, 0)
    turn_wait_send(own, inbox1, relay1, 0)
    halo_wait(sym, 0)

    half = (nI + 2) // 2

    @pl.loop(0, 2)
    def _(t):
        k0 = t * half
        pre = conv(sym, k0, half, nP + 1, 0) + bias1
        value, rise = gelu_and_slope(pre)
        hid[pl.ds(k0, half)] = value.astype(BF16).reshape(half, nP + 1, PHASES, L)
        slope[pl.ds(k0, half)] = rise.reshape(half, nP + 1, PHASES, L)

    clear_outside(hid)

    @pl.loop(0, NQ)
    def _(t):
        k0 = t * QB
        pre = conv(hid, k0, QB, nP, 1) + bias2
        value, rise = gelu_and_slope(pre)
        size = (QB, nP, PHASES, L)
        base = sym[pl.ds(k0 + 2, QB)][:, 1 : nP + 1].astype(F32)
        fresh[pl.ds(k0, QB)] = (base + value.reshape(size)).astype(BF16)
        pull = cot[pl.ds(k0, QB)].astype(F32) * rise.reshape(size)
        g2[pl.ds(k0 + 2, QB), 1 : nP + 1] = pull.astype(BF16)

    halo_start(g2, 1)
    leave(fresh, out_ref)
    halo_wait(g2, 1)

    @pl.loop(0, 2)
    def _(t):
        k0 = t * half
        pulled = conv(g2, k0, half, nP + 1, 2).reshape(half, nP + 1, PHASES, L)
        g1[pl.ds(k0, half)] = (pulled * slope[pl.ds(k0, half)]).astype(BF16)

    clear_outside(g1)

    for q in range(NQ):
        k0 = q * QB
        total = conv(g1, k0, QB, nP, 3).reshape(QB, nP, PHASES, L)
        gsym[pl.ds(k0, QB)] = (cot[pl.ds(k0, QB)].astype(F32) + total).astype(BF16)
        turn_start(gsym, inbox2, relay2, 1, [q])
    turn_relay(inbox2, relay2, 1)

    for q in range(NQ):
        turn_wait_recv(gsym, inbox2, 1, q)
        got = turned(inbox2, q, phase, lanes)
        for jp in range(nP):
            for b in range(2):
                i = q * QB + 2 * jp + b
                total = gsym[i].astype(F32) + got[:, jp, :, b * L : (b + 1) * L].astype(F32)
                fresh[i] = total.astype(BF16)
    turn_wait_send(gsym, inbox2, relay2, 1)
    leave(fresh, grad_ref)


def per_device(rows_axis, cols_axis, feature, w1, b1, w2, b2, cotangent):
    TR, TC, C = feature.shape
    nI, nP = TR // STEP, TC // (2 * STEP)
    QB, NQ, L = TC // STEP, TR // TC, 2 * C
    turned = lambda x: jnp.transpose(x, (1, 2, 0))
    image = lambda i, p: pltpu.VMEM((i, p, PHASES, L), BF16)
    vmem = pl.BlockSpec(memory_space=pltpu.VMEM)
    out = jax.ShapeDtypeStruct((TC, C, TR), BF16)
    res = pl.pallas_call(
        functools.partial(kernel, rows_axis, cols_axis),
        out_shape=(out, out),
        in_specs=[vmem] * 6,
        out_specs=(vmem, vmem),
        scratch_shapes=[
            pltpu.VMEM((nI * PHASES, STEP * TR), BF16),
            image(nI, nP),
            image(nI, nP),
            image(nI + 4, nP + 2),
            image(nI + 2, nP + 1),
            image(nI + 4, nP + 2),
            image(nI + 2, nP + 1),
            image(nI, nP),
            image(nI, nP),
            pltpu.VMEM((nI + 2, nP + 1, PHASES, L), F32),
            pltpu.VMEM((4, 12 * C, L), BF16),
            pltpu.VMEM((NQ, QB, nP, PHASES, L), BF16),
            pltpu.VMEM((NQ, QB, nP, PHASES, L), BF16),
            pltpu.VMEM((len(ROUTES), SLOTS, 2, QB // 2, nP, PHASES, L), BF16),
            pltpu.VMEM((len(ROUTES), SLOTS, 2, QB // 2, nP, PHASES, L), BF16),
            pltpu.SemaphoreType.DMA((2, 8)),
            pltpu.SemaphoreType.DMA((2, 8)),
            pltpu.SemaphoreType.DMA((2, NQ, 2)),
            pltpu.SemaphoreType.DMA((2, NQ, 2)),
            pltpu.SemaphoreType.DMA((2, len(ROUTES), SLOTS, 2)),
            pltpu.SemaphoreType.DMA((2, len(ROUTES), SLOTS, 2)),
        ],
        compiler_params=pltpu.CompilerParams(
            collective_id=0, has_side_effects=True, vmem_limit_bytes=60000000
        ),
    )(turned(feature), w1, b1.reshape(1, C), w2, b2.reshape(1, C), turned(cotangent))
    return tuple(jnp.transpose(x, (2, 0, 1)) for x in res)


def solution(mesh):
    specs = P("row", "col", None)
    return jax.shard_map(
        functools.partial(per_device, mesh.shape["row"], mesh.shape["col"]),
        mesh=mesh,
        in_specs=(specs, P(), P(), P(), P(), specs),
        out_specs=(specs, specs),
        check_vma=False,
    )
```

```python
import functools

import jax
import jax.numpy as jnp
from jax import lax
from jax.experimental import pallas as pl
from jax.experimental.pallas import tpu as pltpu
from jax.sharding import PartitionSpec as P

MESH = pl.DeviceIdType.MESH
STEP = 4
PHASES = STEP * STEP
F32 = jnp.float32
BF16 = jnp.bfloat16
ROOT_HALF = 0.7071067811865476
INV_ROOT_TAU = 0.3989422804014327
SLOTS = 16
PARTS = 1
ROUTES = ((1224305661, 568855674),)
DIRECTIONS = [(-1, 0), (1, 0), (0, -1), (0, 1), (-1, -1), (-1, 1), (1, -1), (1, 1)]
NT = (((1,), (1,)), ((), ()))
TN = (((0,), (0,)), ((), ()))


def iota2(shape, dim):
    return lax.broadcasted_iota(jnp.int32, shape, dim)


def dot(a, b, dims=None):
    if dims is None:
        return jnp.dot(a, b, preferred_element_type=F32)
    return lax.dot_general(a, b, dims, preferred_element_type=F32)


def gelu_and_slope(v):
    half_cdf = 0.5 * (1.0 + lax.erf(v * ROOT_HALF))
    return v * half_cdf, half_cdf + v * jnp.exp(-0.5 * v * v) * INV_ROOT_TAU


def gelu_value(v):
    return 0.5 * v * (1.0 + lax.erf(v * ROOT_HALF))


def kernel(
    rows_axis,
    cols_axis,
    feature_hbm,
    w_first_hbm,
    b_first_hbm,
    w_second_hbm,
    b_second_hbm,
    cotangent_hbm,
    out_ref,
    grad_ref,
    feature,
    w_first,
    b_first,
    w_second,
    b_second,
    cotangent,
    load_sem,
    entry,
    own,
    cot,
    sym,
    hid,
    g2,
    g1,
    gsym,
    fresh,
    slope,
    packed,
    inbox1,
    inbox2,
    relay1,
    relay2,
    halo_send,
    halo_recv,
    turn_send,
    turn_recv,
    relay_send,
    relay_recv,
):
    C = w_first.shape[-1]
    TC, _, TR = feature.shape
    nI, nP = TR // STEP, TC // (2 * STEP)
    QB = TC // STEP
    NQ = TR // TC
    L = 2 * C
    r, c = lax.axis_index("row"), lax.axis_index("col")

    def partner(q):
        return (c // NQ, r * NQ + q)

    def is_self(q):
        return jnp.logical_and(c // NQ == r, r * NQ + q == c)

    def same(a, b):
        return jnp.logical_and(a[0] == b[0], a[1] == b[1])

    me = (r, c)

    def via_xy(s, q):
        return ((s[0] // 4) * 4 + (s[1] // 4) % 4, (s[0] // 2) * 8 + s[1] % 8)

    def via_xy_slot(q):
        return ((c // 16) * 2 + r % 2) * 4 + q

    def via_xy_source(n):
        x = 2 * (n // 8) + (r % 4) // 2
        y = 2 * ((c // 8) % 2) + (n // 4) % 2
        return ((r // 4) * 4 + y, x * 8 + c % 8), n % 4

    kinds = [
        (
            via_xy,
            via_xy_slot,
            via_xy_source,
            jnp.logical_and(r // 4 == c // 16, (c % 8) // 4 == r % 2),
            [((c // 16) * 4 + r % 4, (c // 8) * 8 + (r % 2) * 4 + k) for k in range(4)],
            [via_xy_source(n)[0] for n in range(0, SLOTS, 4)],
            [via_xy(me, 0)],
            16,
            lambda m: ((m % 4) * 4 + m // (4 * PARTS), (m // 4) % PARTS),
        ),
    ]

    def taken(kind, part, s, q):
        x1, x0, y1, y0 = s[1] // 16, (s[1] // 8) % 2, (s[0] % 4) // 2, s[0] % 2
        z2, z1, z0, q1 = (s[1] % 8) // 4, (s[1] // 2) % 2, s[0] // 4, q // 2
        differ = lambda a, b: (a + b) % 2
        at = y0 + 2 * z2 + 4 * differ(x1, z0) + 8 * differ(x0, y1) + 16 * differ(z1, q1)
        words = [jnp.int32(word) for word in ROUTES[kind]]
        word = words[q % 2] if isinstance(q, int) else jnp.where(q % 2 == 0, *words)
        w = kinds[kind][0](s, q)
        target = (s[1] // NQ, s[0] * NQ + q)
        aside = jnp.logical_not(jnp.logical_or(same(w, s), same(w, target)))
        return jnp.logical_and(aside, lax.shift_right_logical(word, at) % 2 == 1)

    def exists(d):
        dr, dc = d
        ok = None
        for delta, pos, size in ((dr, r, rows_axis), (dc, c, cols_axis)):
            if delta == -1:
                cond = pos > 0
            elif delta == 1:
                cond = pos < size - 1
            else:
                continue
            ok = cond if ok is None else jnp.logical_and(ok, cond)
        return ok

    loads = [
        pltpu.make_async_copy(a, b, load_sem.at[i])
        for i, (a, b) in enumerate(
            (
                (feature_hbm, feature),
                (cotangent_hbm, cotangent),
                (w_first_hbm, w_first),
                (w_second_hbm, w_second),
                (b_first_hbm, b_first),
                (b_second_hbm, b_second),
            )
        )
    ]
    for load in loads:
        load.start()

    for img in (sym, g2):
        img[0:2] = jnp.zeros((2, nP + 2, PHASES, L), BF16)
        img[nI + 2 : nI + 4] = jnp.zeros((2, nP + 2, PHASES, L), BF16)
        img[:, 0:1] = jnp.zeros((nI + 4, 1, PHASES, L), BF16)
        img[:, nP + 1 : nP + 2] = jnp.zeros((nI + 4, 1, PHASES, L), BF16)

    barrier = pltpu.get_barrier_semaphore()
    expected = jnp.int32(0)
    for q in range(NQ):
        other = jnp.logical_not(is_self(q))
        expected = expected + other.astype(jnp.int32)

        @pl.when(other)
        def _():
            pl.semaphore_signal(barrier, inc=1, device_id=partner(q), device_id_type=MESH)

    def greet(other):
        @pl.when(jnp.logical_not(same(other, me)))
        def _():
            pl.semaphore_signal(barrier, inc=1, device_id=other, device_id_type=MESH)

    for _, _, _, relaying, relays, sources, firsts, targets, _ in kinds:
        greeted = jnp.int32(targets)
        for other in relays:
            greet(other)
            greeted = greeted - same(other, me).astype(jnp.int32)
        for other in firsts:
            expected = expected + jnp.logical_not(same(other, me)).astype(jnp.int32)
        expected = expected + jnp.where(relaying, greeted, 0)

        @pl.when(relaying)
        def _():
            for other in sources:
                greet(other)

    for d in DIRECTIONS:
        here = exists(d)
        expected = expected + here.astype(jnp.int32)

        @pl.when(here)
        def _():
            pl.semaphore_signal(
                barrier, inc=1, device_id=(r + d[0], c + d[1]), device_id_type=MESH
            )

    shape = (nI * PHASES, STEP * TR)
    at = iota2(shape, 0)
    target = ((at // STEP) % STEP) * TR + (at // PHASES) * STEP + at % STEP
    entry[...] = jnp.where(iota2(shape, 1) == target, 1.0, 0.0).astype(BF16)

    def enter(src, dst):
        for jp in range(nP):
            base = jp * 2 * STEP
            blocks = [
                jnp.concatenate([src[base + s], src[base + STEP + s]], axis=0) for s in range(STEP)
            ]
            res = dot(entry[...], jnp.concatenate(blocks, axis=1), NT)
            dst[:, jp] = res.astype(BF16).reshape(nI, PHASES, L)

    def leave(src, dst):
        for jp in range(nP):
            base = jp * 2 * STEP
            res = dot(src[:, jp].reshape(nI * PHASES, L), entry[...], TN).astype(BF16)
            for b in range(2):
                for s in range(STEP):
                    dst[base + STEP * b + s] = res[b * C : (b + 1) * C, s * TR : (s + 1) * TR]

    half_rows = QB // PARTS

    def part_rows(part):
        return pl.ds(part * half_rows, half_rows)

    def block(src, q, part):
        return src.at[pl.ds(q * QB + part * half_rows, half_rows)]

    def direct_copy(src, inbox, k, q, part):
        slot = lax.rem(c, NQ)
        return pltpu.make_async_remote_copy(
            src_ref=block(src, q, part),
            dst_ref=inbox.at[slot, part_rows(part)],
            send_sem=turn_send.at[k, q, part],
            recv_sem=turn_recv.at[k, slot, part],
            device_id=partner(q),
            device_id_type=MESH,
        )

    def first_copy(src, relay, k, kind, q, part):
        slot = kinds[kind][1](q)
        return pltpu.make_async_remote_copy(
            src_ref=block(src, q, part),
            dst_ref=relay.at[kind, slot, part],
            send_sem=turn_send.at[k, q, part],
            recv_sem=relay_recv.at[k, kind, slot, part],
            device_id=kinds[kind][0](me, q),
            device_id_type=MESH,
        )

    def onward_copy(inbox, relay, k, kind, n, part):
        s, q = kinds[kind][2](n)
        slot = lax.rem(s[1], NQ)
        return pltpu.make_async_remote_copy(
            src_ref=relay.at[kind, n, part],
            dst_ref=inbox.at[slot, part_rows(part)],
            send_sem=relay_send.at[k, kind, n, part],
            recv_sem=turn_recv.at[k, slot, part],
            device_id=(s[1] // NQ, s[0] * NQ + q),
            device_id_type=MESH,
        )

    def local_copy(src, inbox, k, q, part):
        return pltpu.make_async_copy(
            block(src, q, part), inbox.at[q, part_rows(part)], turn_recv.at[k, q, part]
        )

    def way(q, part):
        by = [taken(kind, part, me, q) for kind in range(len(kinds))]
        straight = jnp.logical_not(is_self(q))
        for one in by:
            straight = jnp.logical_and(straight, jnp.logical_not(one))
        return by, straight

    ways = {(q, part): way(q, part) for q in range(NQ) for part in range(PARTS)}

    def turn_start(src, inbox, relay, k, qs):
        for q in qs:
            for part in range(PARTS):
                for kind, one in enumerate(ways[q, part][0]):

                    @pl.when(one)
                    def _():
                        first_copy(src, relay, k, kind, q, part).start()

        for q in qs:
            for part in range(PARTS):

                @pl.when(ways[q, part][1])
                def _():
                    direct_copy(src, inbox, k, q, part).start()

            @pl.when(is_self(q))
            def _():
                for part in range(PARTS):
                    local_copy(src, inbox, k, q, part).start()

    def slots_do(act):
        @pl.loop(0, PARTS * SLOTS)
        def _(m):
            for kind, entry_of in enumerate(kinds):
                n, part = entry_of[-1](m)
                s, q = entry_of[2](n)

                @pl.when(jnp.logical_and(entry_of[3], taken(kind, part, s, q)))
                def _():
                    act(kind, n, part)

    def turn_relay(inbox, relay, k):
        def act(kind, n, part):
            at = relay.at[kind, n, part]
            pltpu.make_async_copy(at, at, relay_recv.at[k, kind, n, part]).wait()
            onward_copy(inbox, relay, k, kind, n, part).start()

        slots_do(act)

    def turn_wait_recv(src, inbox, k, q):
        for part in range(PARTS):
            local_copy(src, inbox, k, q, part).wait()

    def turn_wait_send(src, inbox, relay, k):
        for q in range(NQ):
            for part in range(PARTS):

                @pl.when(jnp.logical_not(is_self(q)))
                def _():
                    direct_copy(src, inbox, k, q, part).wait_send()

        def act(kind, n, part):
            onward_copy(inbox, relay, k, kind, n, part).wait_send()

        slots_do(act)

    def swap_matrices():
        n = PHASES * 8
        x, y = iota2((n, n), 0), iota2((n, n), 1)
        flipped = (x // PHASES) * PHASES + (x % STEP) * STEP + (x // STEP) % STEP
        phase = jnp.where(y == flipped, 1.0, 0.0).astype(BF16)
        m = 2 * L
        x, y = iota2((m, m), 0), iota2((m, m), 1)
        flipped = ((x // C) % 2) * L + (x // L) * C + x % C
        lanes = jnp.where(y == flipped, 1.0, 0.0).astype(BF16)
        return phase, lanes

    def turned(inbox, q, phase, lanes):
        got = inbox[q].reshape(nP, 2, nP, PHASES, L)
        pair = jnp.concatenate([got[:, 0], got[:, 1]], axis=-1).reshape(nP * nP * PHASES, 2 * L)
        swapped = dot(pair, lanes).astype(BF16)
        n = phase.shape[0]
        parts = [
            dot(phase, swapped[i * n : (i + 1) * n]).astype(BF16)
            for i in range(nP * nP * PHASES // n)
        ]
        return jnp.concatenate(parts, axis=0).reshape(nP, nP, PHASES, 2 * L)

    pieces = [(-1, 0, 0), (-1, -1, 0), (-1, 1, 0), (1, 0, 0), (1, -1, 0), (1, 1, 0)]
    pieces += [(0, dc, part) for part in range(2) for dc in (-1, 1)]

    def halo_copy(img, k, n):
        dr, dc, part = pieces[n]
        half = nI // 2
        rows = {-1: (2, nI + 2, 2), 0: (2 + part * half,) * 2 + (half,), 1: (nI, 0, 2)}[dr]
        cols = {-1: (1, nP + 1, 1), 0: (1, 1, nP), 1: (nP, 0, 1)}[dc]
        return pltpu.make_async_remote_copy(
            src_ref=img.at[pl.ds(rows[0], rows[2]), pl.ds(cols[0], cols[2])],
            dst_ref=img.at[pl.ds(rows[1], rows[2]), pl.ds(cols[1], cols[2])],
            send_sem=halo_send.at[k, n],
            recv_sem=halo_recv.at[k, n],
            device_id=(r + dr, c + dc),
            device_id_type=MESH,
        )

    def halo_start(img, k, q):
        last = {0: (0, 1, 2), NQ // 2 - 1: (6, 7), NQ - 1: (8, 9, 3, 4, 5)}
        for n in last.get(q, ()):

            @pl.when(exists(pieces[n][:2]))
            def _():
                halo_copy(img, k, n).start()

    def halo_wait(img, k):
        for n, (dr, dc, _) in enumerate(pieces):

            @pl.when(exists((-dr, -dc)))
            def _():
                halo_copy(img, k, n).wait_recv()

            @pl.when(exists((dr, dc)))
            def _():
                halo_copy(img, k, n).wait_send()

    def conv(src, k0, count, p0, pairs, which):
        taps = []
        for dy in range(3):
            got = src[pl.ds(k0 + dy, count), p0 : p0 + pairs + 1]
            for side in range(2):
                taps.append(got[:, side : side + pairs].reshape(count * pairs * PHASES, L))
        return dot(jnp.concatenate(taps, axis=1), packed[which])

    inside = [(2 + t * (nI - 2) // 2, (nI - 2) // 2, 1, nP - 1) for t in range(2)]
    around = [(0, 2, 0, nP + 1), (nI, 2, 0, nP + 1), (2, nI - 2, 0, 1), (2, nI - 2, nP, 1)]

    def clear_outside(img):
        @pl.when(r == 0)
        def _():
            img[0] = jnp.zeros((nP + 1, PHASES, L), BF16)

        @pl.when(r == rows_axis - 1)
        def _():
            img[nI + 1] = jnp.zeros((nP + 1, PHASES, L), BF16)

        @pl.when(c == 0)
        def _():
            img[:, 0, :, 0:C] = jnp.zeros((nI + 2, PHASES, C), BF16)

        @pl.when(c == cols_axis - 1)
        def _():
            img[:, nP, :, C:L] = jnp.zeros((nI + 2, PHASES, C), BF16)

    loads[0].wait()
    enter(feature, own)
    pl.semaphore_wait(barrier, expected)
    turn_start(own, inbox1, relay1, 0, range(NQ))
    turn_relay(inbox1, relay1, 0)

    for load in loads[1:]:
        load.wait()
    enter(cotangent, cot)
    eye = jnp.where(iota2((C, C), 0) == iota2((C, C), 1), 1.0, 0.0).astype(BF16)
    nothing = jnp.zeros((C, C), BF16)
    for which, w, back in ((0, w_first, 0), (1, w_second, 0), (2, w_second, 1), (3, w_first, 1)):
        for dy in range(3):
            tap = [
                dot(eye, w[2 - dy, 2 - kx], NT).astype(BF16) if back else w[dy, kx]
                for kx in range(3)
            ]
            for a in range(4):
                left = tap[a] if a < 3 else nothing
                right = tap[a - 1] if a > 0 else nothing
                packed[which, pl.ds(dy * 4 * C + a * C, C)] = jnp.concatenate([left, right], axis=1)
    bias1 = jnp.concatenate([b_first[...], b_first[...]], axis=1)
    bias2 = jnp.concatenate([b_second[...], b_second[...]], axis=1)

    phase, lanes = swap_matrices()
    for q in range(NQ):
        turn_wait_recv(own, inbox1, 0, q)
        got = turned(inbox1, q, phase, lanes)
        for jp in range(nP):
            for b in range(2):
                i = q * QB + 2 * jp + b
                total = own[i].astype(F32) + got[:, jp, :, b * L : (b + 1) * L].astype(F32)
                sym[i + 2, 1 : nP + 1] = total.astype(BF16)
        halo_start(sym, 0, q)

    def first_layer(k0, count, p0, pairs):
        pre = conv(sym, k0, count, p0, pairs, 0) + bias1
        value, rise = gelu_and_slope(pre)
        size = (count, pairs, PHASES, L)
        hid[pl.ds(k0, count), p0 : p0 + pairs] = value.astype(BF16).reshape(size)
        slope[pl.ds(k0, count), p0 : p0 + pairs] = rise.reshape(size)

    for box in inside:
        first_layer(*box)
    turn_wait_send(own, inbox1, relay1, 0)
    halo_wait(sym, 0)
    for box in around:
        first_layer(*box)
    clear_outside(hid)

    for q in range(NQ):
        k0 = q * QB
        pre = conv(hid, k0, QB, 0, nP, 1) + bias2
        value, rise = gelu_and_slope(pre)
        size = (QB, nP, PHASES, L)
        base = sym[pl.ds(k0 + 2, QB), 1 : nP + 1].astype(F32)
        fresh[pl.ds(k0, QB)] = (base + value.reshape(size)).astype(BF16)
        pull = cot[pl.ds(k0, QB)].astype(F32) * rise.reshape(size)
        g2[pl.ds(k0 + 2, QB), 1 : nP + 1] = pull.astype(BF16)
        halo_start(g2, 1, q)

    def first_pull(k0, count, p0, pairs):
        size = (count, pairs, PHASES, L)
        pulled = conv(g2, k0, count, p0, pairs, 2).reshape(size)
        rise = slope[pl.ds(k0, count), p0 : p0 + pairs]
        g1[pl.ds(k0, count), p0 : p0 + pairs] = (pulled * rise).astype(BF16)

    for box in inside:
        first_pull(*box)
    leave(fresh, out_ref)
    halo_wait(g2, 1)
    for box in around:
        first_pull(*box)

    clear_outside(g1)

    for q in range(NQ):
        k0 = q * QB
        total = conv(g1, k0, QB, 0, nP, 3).reshape(QB, nP, PHASES, L)
        gsym[pl.ds(k0, QB)] = (cot[pl.ds(k0, QB)].astype(F32) + total).astype(BF16)
        turn_start(gsym, inbox2, relay2, 1, [q])
    turn_relay(inbox2, relay2, 1)

    for q in range(NQ):
        turn_wait_recv(gsym, inbox2, 1, q)
        got = turned(inbox2, q, phase, lanes)
        for jp in range(nP):
            for b in range(2):
                i = q * QB + 2 * jp + b
                total = gsym[i].astype(F32) + got[:, jp, :, b * L : (b + 1) * L].astype(F32)
                fresh[i] = total.astype(BF16)
    turn_wait_send(gsym, inbox2, relay2, 1)
    leave(fresh, grad_ref)


def per_device(rows_axis, cols_axis, feature, w1, b1, w2, b2, cotangent):
    TR, TC, C = feature.shape
    nI, nP = TR // STEP, TC // (2 * STEP)
    QB, NQ, L = TC // STEP, TR // TC, 2 * C
    turned = lambda x: jnp.transpose(x, (1, 2, 0))
    image = lambda i, p: pltpu.VMEM((i, p, PHASES, L), BF16)
    vmem = pl.BlockSpec(memory_space=pltpu.VMEM)
    out = jax.ShapeDtypeStruct((TC, C, TR), BF16)
    res = pl.pallas_call(
        functools.partial(kernel, rows_axis, cols_axis),
        out_shape=(out, out),
        in_specs=[pl.BlockSpec(memory_space=pltpu.HBM)] * 6,
        out_specs=(vmem, vmem),
        scratch_shapes=[
            pltpu.VMEM((TC, C, TR), BF16),
            pltpu.VMEM(w1.shape, BF16),
            pltpu.VMEM((1, C), F32),
            pltpu.VMEM(w2.shape, BF16),
            pltpu.VMEM((1, C), F32),
            pltpu.VMEM((TC, C, TR), BF16),
            pltpu.SemaphoreType.DMA((6,)),
            pltpu.VMEM((nI * PHASES, STEP * TR), BF16),
            image(nI, nP),
            image(nI, nP),
            image(nI + 4, nP + 2),
            image(nI + 2, nP + 1),
            image(nI + 4, nP + 2),
            image(nI + 2, nP + 1),
            image(nI, nP),
            image(nI, nP),
            pltpu.VMEM((nI + 2, nP + 1, PHASES, L), F32),
            pltpu.VMEM((4, 12 * C, L), BF16),
            pltpu.VMEM((NQ, QB, nP, PHASES, L), BF16),
            pltpu.VMEM((NQ, QB, nP, PHASES, L), BF16),
            pltpu.VMEM((len(ROUTES), SLOTS, PARTS, QB // PARTS, nP, PHASES, L), BF16),
            pltpu.VMEM((len(ROUTES), SLOTS, PARTS, QB // PARTS, nP, PHASES, L), BF16),
            pltpu.SemaphoreType.DMA((2, 10)),
            pltpu.SemaphoreType.DMA((2, 10)),
            pltpu.SemaphoreType.DMA((2, NQ, PARTS)),
            pltpu.SemaphoreType.DMA((2, NQ, PARTS)),
            pltpu.SemaphoreType.DMA((2, len(ROUTES), SLOTS, PARTS)),
            pltpu.SemaphoreType.DMA((2, len(ROUTES), SLOTS, PARTS)),
        ],
        compiler_params=pltpu.CompilerParams(
            collective_id=0, has_side_effects=True, vmem_limit_bytes=60000000
        ),
    )(turned(feature), w1, b1.reshape(1, C), w2, b2.reshape(1, C), turned(cotangent))
    return tuple(jnp.transpose(x, (2, 0, 1)) for x in res)


def solution(mesh):
    specs = P("row", "col", None)
    return jax.shard_map(
        functools.partial(per_device, mesh.shape["row"], mesh.shape["col"]),
        mesh=mesh,
        in_specs=(specs, P(), P(), P(), P(), specs),
        out_specs=(specs, specs),
        check_vma=False,
    )
```

```python
import functools

import jax
import jax.numpy as jnp
from jax import lax
from jax.experimental import pallas as pl
from jax.experimental.pallas import tpu as pltpu
from jax.sharding import PartitionSpec as P

MESH = pl.DeviceIdType.MESH
STEP = 4
PHASES = STEP * STEP
F32 = jnp.float32
BF16 = jnp.bfloat16
ROOT_HALF = 0.7071067811865476
INV_ROOT_TAU = 0.3989422804014327
SLOTS = 16
PARTS = 1
ROUTES = ((-638580491, 548734887),)
DIRECTIONS = [(-1, 0), (1, 0), (0, -1), (0, 1), (-1, -1), (-1, 1), (1, -1), (1, 1)]
NT = (((1,), (1,)), ((), ()))
TN = (((0,), (0,)), ((), ()))


def iota2(shape, dim):
    return lax.broadcasted_iota(jnp.int32, shape, dim)


def dot(a, b, dims=None):
    if dims is None:
        return jnp.dot(a, b, preferred_element_type=F32)
    return lax.dot_general(a, b, dims, preferred_element_type=F32)


def gelu_and_slope(v):
    half_cdf = 0.5 * (1.0 + lax.erf(v * ROOT_HALF))
    return v * half_cdf, half_cdf + v * jnp.exp(-0.5 * v * v) * INV_ROOT_TAU


def gelu_value(v):
    return 0.5 * v * (1.0 + lax.erf(v * ROOT_HALF))


def kernel(
    rows_axis,
    cols_axis,
    feature_hbm,
    w_first_hbm,
    b_first_hbm,
    w_second_hbm,
    b_second_hbm,
    cotangent_hbm,
    out_ref,
    grad_ref,
    feature,
    w_first,
    b_first,
    w_second,
    b_second,
    cotangent,
    load_sem,
    entry,
    own,
    cot,
    sym,
    hid,
    g2,
    g1,
    gsym,
    fresh,
    slope,
    packed,
    inbox1,
    inbox2,
    relay1,
    relay2,
    halo_send,
    halo_recv,
    turn_send,
    turn_recv,
    relay_send,
    relay_recv,
):
    C = w_first.shape[-1]
    TC, _, TR = feature.shape
    nI, nP = TR // STEP, TC // (2 * STEP)
    QB = TC // STEP
    NQ = TR // TC
    L = 2 * C
    r, c = lax.axis_index("row"), lax.axis_index("col")

    def partner(q):
        return (c // NQ, r * NQ + q)

    def is_self(q):
        return jnp.logical_and(c // NQ == r, r * NQ + q == c)

    def same(a, b):
        return jnp.logical_and(a[0] == b[0], a[1] == b[1])

    me = (r, c)

    def via_xy(s, q):
        return ((s[0] // 4) * 4 + (s[1] // 4) % 4, (s[0] // 2) * 8 + s[1] % 8)

    def via_xy_slot(q):
        return ((c // 16) * 2 + r % 2) * 4 + q

    def via_xy_source(n):
        x = 2 * (n // 8) + (r % 4) // 2
        y = 2 * ((c // 8) % 2) + (n // 4) % 2
        return ((r // 4) * 4 + y, x * 8 + c % 8), n % 4

    kinds = [
        (
            via_xy,
            via_xy_slot,
            via_xy_source,
            jnp.logical_and(r // 4 == c // 16, (c % 8) // 4 == r % 2),
            [((c // 16) * 4 + r % 4, (c // 8) * 8 + (r % 2) * 4 + k) for k in range(4)],
            [via_xy_source(n)[0] for n in range(0, SLOTS, 4)],
            [via_xy(me, 0)],
            16,
            lambda m: ((m % 4) * 4 + m // (4 * PARTS), (m // 4) % PARTS),
        ),
    ]

    def taken(kind, part, s, q):
        x1, x0, y1, y0 = s[1] // 16, (s[1] // 8) % 2, (s[0] % 4) // 2, s[0] % 2
        z2, z1, z0, q1 = (s[1] % 8) // 4, (s[1] // 2) % 2, s[0] // 4, q // 2
        differ = lambda a, b: (a + b) % 2
        at = z1 + 2 * q1 + 4 * differ(x1, z0) + 8 * differ(x0, y1) + 16 * differ(y0, z2)
        words = [jnp.int32(word) for word in ROUTES[kind]]
        word = words[q % 2] if isinstance(q, int) else jnp.where(q % 2 == 0, *words)
        w = kinds[kind][0](s, q)
        target = (s[1] // NQ, s[0] * NQ + q)
        aside = jnp.logical_not(jnp.logical_or(same(w, s), same(w, target)))
        return jnp.logical_and(aside, lax.shift_right_logical(word, at) % 2 == 1)

    def exists(d):
        dr, dc = d
        ok = None
        for delta, pos, size in ((dr, r, rows_axis), (dc, c, cols_axis)):
            if delta == -1:
                cond = pos > 0
            elif delta == 1:
                cond = pos < size - 1
            else:
                continue
            ok = cond if ok is None else jnp.logical_and(ok, cond)
        return ok

    loads = [
        pltpu.make_async_copy(a, b, load_sem.at[i])
        for i, (a, b) in enumerate(
            (
                (feature_hbm, feature),
                (cotangent_hbm, cotangent),
                (w_first_hbm, w_first),
                (w_second_hbm, w_second),
                (b_first_hbm, b_first),
                (b_second_hbm, b_second),
            )
        )
    ]
    for load in loads:
        load.start()

    for img in (sym, g2):
        img[0:2] = jnp.zeros((2, nP + 2, PHASES, L), BF16)
        img[nI + 2 : nI + 4] = jnp.zeros((2, nP + 2, PHASES, L), BF16)
        img[:, 0:1] = jnp.zeros((nI + 4, 1, PHASES, L), BF16)
        img[:, nP + 1 : nP + 2] = jnp.zeros((nI + 4, 1, PHASES, L), BF16)

    barrier = pltpu.get_barrier_semaphore()
    expected = jnp.int32(0)
    for q in range(NQ):
        other = jnp.logical_not(is_self(q))
        expected = expected + other.astype(jnp.int32)

        @pl.when(other)
        def _():
            pl.semaphore_signal(barrier, inc=1, device_id=partner(q), device_id_type=MESH)

    def greet(other):
        @pl.when(jnp.logical_not(same(other, me)))
        def _():
            pl.semaphore_signal(barrier, inc=1, device_id=other, device_id_type=MESH)

    for _, _, _, relaying, relays, sources, firsts, targets, _ in kinds:
        greeted = jnp.int32(targets)
        for other in relays:
            greet(other)
            greeted = greeted - same(other, me).astype(jnp.int32)
        for other in firsts:
            expected = expected + jnp.logical_not(same(other, me)).astype(jnp.int32)
        expected = expected + jnp.where(relaying, greeted, 0)

        @pl.when(relaying)
        def _():
            for other in sources:
                greet(other)

    for d in DIRECTIONS:
        here = exists(d)
        expected = expected + here.astype(jnp.int32)

        @pl.when(here)
        def _():
            pl.semaphore_signal(
                barrier, inc=1, device_id=(r + d[0], c + d[1]), device_id_type=MESH
            )

    shape = (nI * PHASES, STEP * TR)
    at = iota2(shape, 0)
    target = ((at // STEP) % STEP) * TR + (at // PHASES) * STEP + at % STEP
    entry[...] = jnp.where(iota2(shape, 1) == target, 1.0, 0.0).astype(BF16)

    def enter(src, dst):
        for jp in range(nP):
            base = jp * 2 * STEP
            blocks = [
                jnp.concatenate([src[base + s], src[base + STEP + s]], axis=0) for s in range(STEP)
            ]
            res = dot(entry[...], jnp.concatenate(blocks, axis=1), NT)
            dst[:, jp] = res.astype(BF16).reshape(nI, PHASES, L)

    def leave(src, dst):
        for jp in range(nP):
            base = jp * 2 * STEP
            res = dot(src[:, jp].reshape(nI * PHASES, L), entry[...], TN).astype(BF16)
            for b in range(2):
                for s in range(STEP):
                    dst[base + STEP * b + s] = res[b * C : (b + 1) * C, s * TR : (s + 1) * TR]

    half_rows = QB // PARTS

    def part_rows(part):
        return pl.ds(part * half_rows, half_rows)

    def block(src, q, part):
        return src.at[pl.ds(q * QB + part * half_rows, half_rows)]

    def direct_copy(src, inbox, k, q, part):
        slot = lax.rem(c, NQ)
        return pltpu.make_async_remote_copy(
            src_ref=block(src, q, part),
            dst_ref=inbox.at[slot, part_rows(part)],
            send_sem=turn_send.at[k, q, part],
            recv_sem=turn_recv.at[k, slot, part],
            device_id=partner(q),
            device_id_type=MESH,
        )

    def first_copy(src, relay, k, kind, q, part):
        slot = kinds[kind][1](q)
        return pltpu.make_async_remote_copy(
            src_ref=block(src, q, part),
            dst_ref=relay.at[kind, slot, part],
            send_sem=turn_send.at[k, q, part],
            recv_sem=relay_recv.at[k, kind, slot, part],
            device_id=kinds[kind][0](me, q),
            device_id_type=MESH,
        )

    def onward_copy(inbox, relay, k, kind, n, part):
        s, q = kinds[kind][2](n)
        slot = lax.rem(s[1], NQ)
        return pltpu.make_async_remote_copy(
            src_ref=relay.at[kind, n, part],
            dst_ref=inbox.at[slot, part_rows(part)],
            send_sem=relay_send.at[k, kind, n, part],
            recv_sem=turn_recv.at[k, slot, part],
            device_id=(s[1] // NQ, s[0] * NQ + q),
            device_id_type=MESH,
        )

    def local_copy(src, inbox, k, q, part):
        return pltpu.make_async_copy(
            block(src, q, part), inbox.at[q, part_rows(part)], turn_recv.at[k, q, part]
        )

    def way(q, part):
        by = [taken(kind, part, me, q) for kind in range(len(kinds))]
        straight = jnp.logical_not(is_self(q))
        for one in by:
            straight = jnp.logical_and(straight, jnp.logical_not(one))
        return by, straight

    ways = {(q, part): way(q, part) for q in range(NQ) for part in range(PARTS)}

    def turn_start(src, inbox, relay, k, qs):
        for q in qs:
            for part in range(PARTS):
                for kind, one in enumerate(ways[q, part][0]):

                    @pl.when(one)
                    def _():
                        first_copy(src, relay, k, kind, q, part).start()

        for q in qs:
            for part in range(PARTS):

                @pl.when(ways[q, part][1])
                def _():
                    direct_copy(src, inbox, k, q, part).start()

            @pl.when(is_self(q))
            def _():
                for part in range(PARTS):
                    local_copy(src, inbox, k, q, part).start()

    def slots_do(act):
        @pl.loop(0, PARTS * SLOTS)
        def _(m):
            for kind, entry_of in enumerate(kinds):
                n, part = entry_of[-1](m)
                s, q = entry_of[2](n)

                @pl.when(jnp.logical_and(entry_of[3], taken(kind, part, s, q)))
                def _():
                    act(kind, n, part)

    def turn_relay(inbox, relay, k):
        def act(kind, n, part):
            at = relay.at[kind, n, part]
            pltpu.make_async_copy(at, at, relay_recv.at[k, kind, n, part]).wait()
            onward_copy(inbox, relay, k, kind, n, part).start()

        slots_do(act)

    def turn_wait_recv(src, inbox, k, q):
        for part in range(PARTS):
            local_copy(src, inbox, k, q, part).wait()

    def turn_wait_send(src, inbox, relay, k):
        for q in range(NQ):
            for part in range(PARTS):

                @pl.when(jnp.logical_not(is_self(q)))
                def _():
                    direct_copy(src, inbox, k, q, part).wait_send()

        def act(kind, n, part):
            onward_copy(inbox, relay, k, kind, n, part).wait_send()

        slots_do(act)

    def swap_matrices():
        n = PHASES * 8
        x, y = iota2((n, n), 0), iota2((n, n), 1)
        flipped = (x // PHASES) * PHASES + (x % STEP) * STEP + (x // STEP) % STEP
        phase = jnp.where(y == flipped, 1.0, 0.0).astype(BF16)
        m = 2 * L
        x, y = iota2((m, m), 0), iota2((m, m), 1)
        flipped = ((x // C) % 2) * L + (x // L) * C + x % C
        lanes = jnp.where(y == flipped, 1.0, 0.0).astype(BF16)
        return phase, lanes

    def turned(inbox, q, phase, lanes):
        got = inbox[q].reshape(nP, 2, nP, PHASES, L)
        pair = jnp.concatenate([got[:, 0], got[:, 1]], axis=-1).reshape(nP * nP * PHASES, 2 * L)
        swapped = dot(pair, lanes).astype(BF16)
        n = phase.shape[0]
        parts = [
            dot(phase, swapped[i * n : (i + 1) * n]).astype(BF16)
            for i in range(nP * nP * PHASES // n)
        ]
        return jnp.concatenate(parts, axis=0).reshape(nP, nP, PHASES, 2 * L)

    pieces = [(-1, 0, 0), (-1, -1, 0), (-1, 1, 0), (1, 0, 0), (1, -1, 0), (1, 1, 0)]
    pieces += [(0, dc, part) for part in range(2) for dc in (-1, 1)]

    def halo_copy(img, k, n):
        dr, dc, part = pieces[n]
        half = nI // 2
        rows = {-1: (2, nI + 2, 2), 0: (2 + part * half,) * 2 + (half,), 1: (nI, 0, 2)}[dr]
        cols = {-1: (1, nP + 1, 1), 0: (1, 1, nP), 1: (nP, 0, 1)}[dc]
        return pltpu.make_async_remote_copy(
            src_ref=img.at[pl.ds(rows[0], rows[2]), pl.ds(cols[0], cols[2])],
            dst_ref=img.at[pl.ds(rows[1], rows[2]), pl.ds(cols[1], cols[2])],
            send_sem=halo_send.at[k, n],
            recv_sem=halo_recv.at[k, n],
            device_id=(r + dr, c + dc),
            device_id_type=MESH,
        )

    def halo_start(img, k, q):
        last = {0: (0, 1, 2), NQ // 2 - 1: (6, 7), NQ - 1: (8, 9, 3, 4, 5)}
        for n in last.get(q, ()):

            @pl.when(exists(pieces[n][:2]))
            def _():
                halo_copy(img, k, n).start()

    def halo_wait(img, k):
        for n, (dr, dc, _) in enumerate(pieces):

            @pl.when(exists((-dr, -dc)))
            def _():
                halo_copy(img, k, n).wait_recv()

            @pl.when(exists((dr, dc)))
            def _():
                halo_copy(img, k, n).wait_send()

    def conv(src, k0, count, p0, pairs, which):
        taps = []
        for dy in range(3):
            got = src[pl.ds(k0 + dy, count), p0 : p0 + pairs + 1]
            for side in range(2):
                taps.append(got[:, side : side + pairs].reshape(count * pairs * PHASES, L))
        return dot(jnp.concatenate(taps, axis=1), packed[which])

    inside = [(2 + t * (nI - 2) // 2, (nI - 2) // 2, 1, nP - 1) for t in range(2)]
    around = [(0, 2, 0, nP + 1), (nI, 2, 0, nP + 1), (2, nI - 2, 0, 1), (2, nI - 2, nP, 1)]

    def clear_outside(img):
        @pl.when(r == 0)
        def _():
            img[0] = jnp.zeros((nP + 1, PHASES, L), BF16)

        @pl.when(r == rows_axis - 1)
        def _():
            img[nI + 1] = jnp.zeros((nP + 1, PHASES, L), BF16)

        @pl.when(c == 0)
        def _():
            img[:, 0, :, 0:C] = jnp.zeros((nI + 2, PHASES, C), BF16)

        @pl.when(c == cols_axis - 1)
        def _():
            img[:, nP, :, C:L] = jnp.zeros((nI + 2, PHASES, C), BF16)

    loads[0].wait()
    enter(feature, own)
    pl.semaphore_wait(barrier, expected)
    turn_start(own, inbox1, relay1, 0, range(NQ))
    turn_relay(inbox1, relay1, 0)

    for load in loads[1:]:
        load.wait()
    enter(cotangent, cot)
    eye = jnp.where(iota2((C, C), 0) == iota2((C, C), 1), 1.0, 0.0).astype(BF16)
    nothing = jnp.zeros((C, C), BF16)
    for which, w, back in ((0, w_first, 0), (1, w_second, 0), (2, w_second, 1), (3, w_first, 1)):
        for dy in range(3):
            tap = [
                dot(eye, w[2 - dy, 2 - kx], NT).astype(BF16) if back else w[dy, kx]
                for kx in range(3)
            ]
            for a in range(4):
                left = tap[a] if a < 3 else nothing
                right = tap[a - 1] if a > 0 else nothing
                packed[which, pl.ds(dy * 4 * C + a * C, C)] = jnp.concatenate([left, right], axis=1)
    bias1 = jnp.concatenate([b_first[...], b_first[...]], axis=1)
    bias2 = jnp.concatenate([b_second[...], b_second[...]], axis=1)

    phase, lanes = swap_matrices()
    for q in range(NQ):
        turn_wait_recv(own, inbox1, 0, q)
        got = turned(inbox1, q, phase, lanes)
        for jp in range(nP):
            for b in range(2):
                i = q * QB + 2 * jp + b
                total = own[i].astype(F32) + got[:, jp, :, b * L : (b + 1) * L].astype(F32)
                sym[i + 2, 1 : nP + 1] = total.astype(BF16)
        halo_start(sym, 0, q)

    def first_layer(k0, count, p0, pairs):
        pre = conv(sym, k0, count, p0, pairs, 0) + bias1
        value, rise = gelu_and_slope(pre)
        size = (count, pairs, PHASES, L)
        hid[pl.ds(k0, count), p0 : p0 + pairs] = value.astype(BF16).reshape(size)
        slope[pl.ds(k0, count), p0 : p0 + pairs] = rise.reshape(size)

    for box in inside:
        first_layer(*box)
    turn_wait_send(own, inbox1, relay1, 0)
    halo_wait(sym, 0)
    for box in around:
        first_layer(*box)
    clear_outside(hid)

    for q in range(NQ):
        k0 = q * QB
        pre = conv(hid, k0, QB, 0, nP, 1) + bias2
        value, rise = gelu_and_slope(pre)
        size = (QB, nP, PHASES, L)
        base = sym[pl.ds(k0 + 2, QB), 1 : nP + 1].astype(F32)
        fresh[pl.ds(k0, QB)] = (base + value.reshape(size)).astype(BF16)
        pull = cot[pl.ds(k0, QB)].astype(F32) * rise.reshape(size)
        g2[pl.ds(k0 + 2, QB), 1 : nP + 1] = pull.astype(BF16)
        halo_start(g2, 1, q)

    def first_pull(k0, count, p0, pairs):
        size = (count, pairs, PHASES, L)
        pulled = conv(g2, k0, count, p0, pairs, 2).reshape(size)
        rise = slope[pl.ds(k0, count), p0 : p0 + pairs]
        g1[pl.ds(k0, count), p0 : p0 + pairs] = (pulled * rise).astype(BF16)

    for box in inside:
        first_pull(*box)
    leave(fresh, out_ref)
    halo_wait(g2, 1)
    for box in around:
        first_pull(*box)

    clear_outside(g1)

    for q in range(NQ):
        k0 = q * QB
        total = conv(g1, k0, QB, 0, nP, 3).reshape(QB, nP, PHASES, L)
        gsym[pl.ds(k0, QB)] = (cot[pl.ds(k0, QB)].astype(F32) + total).astype(BF16)
        turn_start(gsym, inbox2, relay2, 1, [q])
    turn_relay(inbox2, relay2, 1)

    for q in range(NQ):
        turn_wait_recv(gsym, inbox2, 1, q)
        got = turned(inbox2, q, phase, lanes)
        for jp in range(nP):
            for b in range(2):
                i = q * QB + 2 * jp + b
                total = gsym[i].astype(F32) + got[:, jp, :, b * L : (b + 1) * L].astype(F32)
                fresh[i] = total.astype(BF16)
    turn_wait_send(gsym, inbox2, relay2, 1)
    leave(fresh, grad_ref)


def per_device(rows_axis, cols_axis, feature, w1, b1, w2, b2, cotangent):
    TR, TC, C = feature.shape
    nI, nP = TR // STEP, TC // (2 * STEP)
    QB, NQ, L = TC // STEP, TR // TC, 2 * C
    turned = lambda x: jnp.transpose(x, (1, 2, 0))
    image = lambda i, p: pltpu.VMEM((i, p, PHASES, L), BF16)
    vmem = pl.BlockSpec(memory_space=pltpu.VMEM)
    out = jax.ShapeDtypeStruct((TC, C, TR), BF16)
    res = pl.pallas_call(
        functools.partial(kernel, rows_axis, cols_axis),
        out_shape=(out, out),
        in_specs=[pl.BlockSpec(memory_space=pltpu.HBM)] * 6,
        out_specs=(vmem, vmem),
        scratch_shapes=[
            pltpu.VMEM((TC, C, TR), BF16),
            pltpu.VMEM(w1.shape, BF16),
            pltpu.VMEM((1, C), F32),
            pltpu.VMEM(w2.shape, BF16),
            pltpu.VMEM((1, C), F32),
            pltpu.VMEM((TC, C, TR), BF16),
            pltpu.SemaphoreType.DMA((6,)),
            pltpu.VMEM((nI * PHASES, STEP * TR), BF16),
            image(nI, nP),
            image(nI, nP),
            image(nI + 4, nP + 2),
            image(nI + 2, nP + 1),
            image(nI + 4, nP + 2),
            image(nI + 2, nP + 1),
            image(nI, nP),
            image(nI, nP),
            pltpu.VMEM((nI + 2, nP + 1, PHASES, L), F32),
            pltpu.VMEM((4, 12 * C, L), BF16),
            pltpu.VMEM((NQ, QB, nP, PHASES, L), BF16),
            pltpu.VMEM((NQ, QB, nP, PHASES, L), BF16),
            pltpu.VMEM((len(ROUTES), SLOTS, PARTS, QB // PARTS, nP, PHASES, L), BF16),
            pltpu.VMEM((len(ROUTES), SLOTS, PARTS, QB // PARTS, nP, PHASES, L), BF16),
            pltpu.SemaphoreType.DMA((2, 10)),
            pltpu.SemaphoreType.DMA((2, 10)),
            pltpu.SemaphoreType.DMA((2, NQ, PARTS)),
            pltpu.SemaphoreType.DMA((2, NQ, PARTS)),
            pltpu.SemaphoreType.DMA((2, len(ROUTES), SLOTS, PARTS)),
            pltpu.SemaphoreType.DMA((2, len(ROUTES), SLOTS, PARTS)),
        ],
        compiler_params=pltpu.CompilerParams(
            collective_id=0, has_side_effects=True, vmem_limit_bytes=60000000
        ),
    )(turned(feature), w1, b1.reshape(1, C), w2, b2.reshape(1, C), turned(cotangent))
    return tuple(jnp.transpose(x, (2, 0, 1)) for x in res)


def solution(mesh):
    specs = P("row", "col", None)
    return jax.shard_map(
        functools.partial(per_device, mesh.shape["row"], mesh.shape["col"]),
        mesh=mesh,
        in_specs=(specs, P(), P(), P(), P(), specs),
        out_specs=(specs, specs),
        check_vma=False,
    )
```

```python
import functools

import jax
import jax.numpy as jnp
from jax import lax
from jax.experimental import pallas as pl
from jax.experimental.pallas import tpu as pltpu
from jax.sharding import PartitionSpec as P

MESH = pl.DeviceIdType.MESH
STEP = 4
PHASES = STEP * STEP
F32 = jnp.float32
BF16 = jnp.bfloat16
ROOT_HALF = 0.7071067811865476
INV_ROOT_TAU = 0.3989422804014327
SLOTS = 16
PARTS = 1
ROUTES = ((-638580491, 548734887),)
DIRECTIONS = [(-1, 0), (1, 0), (0, -1), (0, 1), (-1, -1), (-1, 1), (1, -1), (1, 1)]
NT = (((1,), (1,)), ((), ()))
TN = (((0,), (0,)), ((), ()))


def iota2(shape, dim):
    return lax.broadcasted_iota(jnp.int32, shape, dim)


def dot(a, b, dims=None):
    if dims is None:
        return jnp.dot(a, b, preferred_element_type=F32)
    return lax.dot_general(a, b, dims, preferred_element_type=F32)


def gelu_and_slope(v):
    half_cdf = 0.5 * (1.0 + lax.erf(v * ROOT_HALF))
    return v * half_cdf, half_cdf + v * jnp.exp(-0.5 * v * v) * INV_ROOT_TAU


def gelu_value(v):
    return 0.5 * v * (1.0 + lax.erf(v * ROOT_HALF))


def kernel(
    rows_axis,
    cols_axis,
    feature_hbm,
    w_first_hbm,
    b_first_hbm,
    w_second_hbm,
    b_second_hbm,
    cotangent_hbm,
    out_ref,
    grad_ref,
    feature,
    w_first,
    b_first,
    w_second,
    b_second,
    cotangent,
    load_sem,
    entry,
    own,
    cot,
    sym,
    hid,
    g2,
    g1,
    gsym,
    fresh,
    slope,
    packed,
    inbox1,
    inbox2,
    relay1,
    relay2,
    halo_send,
    halo_recv,
    turn_send,
    turn_recv,
    relay_send,
    relay_recv,
):
    C = w_first.shape[-1]
    TC, _, TR = feature.shape
    nI, nP = TR // STEP, TC // (2 * STEP)
    QB = TC // STEP
    NQ = TR // TC
    L = 2 * C
    r, c = lax.axis_index("row"), lax.axis_index("col")

    def partner(q):
        return (c // NQ, r * NQ + q)

    def is_self(q):
        return jnp.logical_and(c // NQ == r, r * NQ + q == c)

    def same(a, b):
        return jnp.logical_and(a[0] == b[0], a[1] == b[1])

    me = (r, c)

    def via_xy(s, q):
        return ((s[0] // 4) * 4 + (s[1] // 4) % 4, (s[0] // 2) * 8 + s[1] % 8)

    def via_xy_slot(q):
        return ((c // 16) * 2 + r % 2) * 4 + q

    def via_xy_source(n):
        x = 2 * (n // 8) + (r % 4) // 2
        y = 2 * ((c // 8) % 2) + (n // 4) % 2
        return ((r // 4) * 4 + y, x * 8 + c % 8), n % 4

    kinds = [
        (
            via_xy,
            via_xy_slot,
            via_xy_source,
            jnp.logical_and(r // 4 == c // 16, (c % 8) // 4 == r % 2),
            [((c // 16) * 4 + r % 4, (c // 8) * 8 + (r % 2) * 4 + k) for k in range(4)],
            [via_xy_source(n)[0] for n in range(0, SLOTS, 4)],
            [via_xy(me, 0)],
            16,
            lambda m: ((m % 4) * 4 + m // (4 * PARTS), (m // 4) % PARTS),
        ),
    ]

    def taken(kind, part, s, q):
        x1, x0, y1, y0 = s[1] // 16, (s[1] // 8) % 2, (s[0] % 4) // 2, s[0] % 2
        z2, z1, z0, q1 = (s[1] % 8) // 4, (s[1] // 2) % 2, s[0] // 4, q // 2
        differ = lambda a, b: (a + b) % 2
        at = z1 + 2 * q1 + 4 * differ(x1, z0) + 8 * differ(x0, y1) + 16 * differ(y0, z2)
        words = [jnp.int32(word) for word in ROUTES[kind]]
        word = words[q % 2] if isinstance(q, int) else jnp.where(q % 2 == 0, *words)
        w = kinds[kind][0](s, q)
        target = (s[1] // NQ, s[0] * NQ + q)
        aside = jnp.logical_not(jnp.logical_or(same(w, s), same(w, target)))
        return jnp.logical_and(aside, lax.shift_right_logical(word, at) % 2 == 1)

    def exists(d):
        dr, dc = d
        ok = None
        for delta, pos, size in ((dr, r, rows_axis), (dc, c, cols_axis)):
            if delta == -1:
                cond = pos > 0
            elif delta == 1:
                cond = pos < size - 1
            else:
                continue
            ok = cond if ok is None else jnp.logical_and(ok, cond)
        return ok

    loads = [
        pltpu.make_async_copy(a, b, load_sem.at[i])
        for i, (a, b) in enumerate(
            (
                (feature_hbm, feature),
                (cotangent_hbm, cotangent),
                (w_first_hbm, w_first),
                (w_second_hbm, w_second),
                (b_first_hbm, b_first),
                (b_second_hbm, b_second),
            )
        )
    ]
    for load in loads:
        load.start()

    for img in (sym, g2):
        img[0:2] = jnp.zeros((2, nP + 2, PHASES, L), BF16)
        img[nI + 2 : nI + 4] = jnp.zeros((2, nP + 2, PHASES, L), BF16)
        img[:, 0:1] = jnp.zeros((nI + 4, 1, PHASES, L), BF16)
        img[:, nP + 1 : nP + 2] = jnp.zeros((nI + 4, 1, PHASES, L), BF16)

    barrier = pltpu.get_barrier_semaphore()
    expected = jnp.int32(0)
    for q in range(NQ):
        other = jnp.logical_not(is_self(q))
        expected = expected + other.astype(jnp.int32)

        @pl.when(other)
        def _():
            pl.semaphore_signal(barrier, inc=1, device_id=partner(q), device_id_type=MESH)

    def greet(other):
        @pl.when(jnp.logical_not(same(other, me)))
        def _():
            pl.semaphore_signal(barrier, inc=1, device_id=other, device_id_type=MESH)

    for _, _, _, relaying, relays, sources, firsts, targets, _ in kinds:
        greeted = jnp.int32(targets)
        for other in relays:
            greet(other)
            greeted = greeted - same(other, me).astype(jnp.int32)
        for other in firsts:
            expected = expected + jnp.logical_not(same(other, me)).astype(jnp.int32)
        expected = expected + jnp.where(relaying, greeted, 0)

        @pl.when(relaying)
        def _():
            for other in sources:
                greet(other)

    for d in DIRECTIONS:
        here = exists(d)
        expected = expected + here.astype(jnp.int32)

        @pl.when(here)
        def _():
            pl.semaphore_signal(
                barrier, inc=1, device_id=(r + d[0], c + d[1]), device_id_type=MESH
            )

    shape = (nI * PHASES, STEP * TR)
    at = iota2(shape, 0)
    target = ((at // STEP) % STEP) * TR + (at // PHASES) * STEP + at % STEP
    entry[...] = jnp.where(iota2(shape, 1) == target, 1.0, 0.0).astype(BF16)

    def enter(src, dst):
        for jp in range(nP):
            base = jp * 2 * STEP
            blocks = [
                jnp.concatenate([src[base + s], src[base + STEP + s]], axis=0) for s in range(STEP)
            ]
            res = dot(entry[...], jnp.concatenate(blocks, axis=1), NT)
            dst[:, jp] = res.astype(BF16).reshape(nI, PHASES, L)

    def leave(src, dst):
        for jp in range(nP):
            base = jp * 2 * STEP
            res = dot(src[:, jp].reshape(nI * PHASES, L), entry[...], TN).astype(BF16)
            for b in range(2):
                for s in range(STEP):
                    dst[base + STEP * b + s] = res[b * C : (b + 1) * C, s * TR : (s + 1) * TR]

    half_rows = QB // PARTS

    def part_rows(part):
        return pl.ds(part * half_rows, half_rows)

    def block(src, q, part):
        return src.at[pl.ds(q * QB + part * half_rows, half_rows)]

    def direct_copy(src, inbox, k, q, part):
        slot = lax.rem(c, NQ)
        return pltpu.make_async_remote_copy(
            src_ref=block(src, q, part),
            dst_ref=inbox.at[slot, part_rows(part)],
            send_sem=turn_send.at[k, q, part],
            recv_sem=turn_recv.at[k, slot, part],
            device_id=partner(q),
            device_id_type=MESH,
        )

    def first_copy(src, relay, k, kind, q, part):
        slot = kinds[kind][1](q)
        return pltpu.make_async_remote_copy(
            src_ref=block(src, q, part),
            dst_ref=relay.at[kind, slot, part],
            send_sem=turn_send.at[k, q, part],
            recv_sem=relay_recv.at[k, kind, slot, part],
            device_id=kinds[kind][0](me, q),
            device_id_type=MESH,
        )

    def onward_copy(inbox, relay, k, kind, n, part):
        s, q = kinds[kind][2](n)
        slot = lax.rem(s[1], NQ)
        return pltpu.make_async_remote_copy(
            src_ref=relay.at[kind, n, part],
            dst_ref=inbox.at[slot, part_rows(part)],
            send_sem=relay_send.at[k, kind, n, part],
            recv_sem=turn_recv.at[k, slot, part],
            device_id=(s[1] // NQ, s[0] * NQ + q),
            device_id_type=MESH,
        )

    def local_copy(src, inbox, k, q, part):
        return pltpu.make_async_copy(
            block(src, q, part), inbox.at[q, part_rows(part)], turn_recv.at[k, q, part]
        )

    def way(q, part):
        by = [taken(kind, part, me, q) for kind in range(len(kinds))]
        straight = jnp.logical_not(is_self(q))
        for one in by:
            straight = jnp.logical_and(straight, jnp.logical_not(one))
        return by, straight

    ways = {(q, part): way(q, part) for q in range(NQ) for part in range(PARTS)}

    def turn_start(src, inbox, relay, k, qs):
        for q in qs:
            for part in range(PARTS):
                for kind, one in enumerate(ways[q, part][0]):

                    @pl.when(one)
                    def _():
                        first_copy(src, relay, k, kind, q, part).start()

        for q in qs:
            for part in range(PARTS):

                @pl.when(ways[q, part][1])
                def _():
                    direct_copy(src, inbox, k, q, part).start()

            @pl.when(is_self(q))
            def _():
                for part in range(PARTS):
                    local_copy(src, inbox, k, q, part).start()

    def slots_do(act):
        @pl.loop(0, PARTS * SLOTS)
        def _(m):
            for kind, entry_of in enumerate(kinds):
                n, part = entry_of[-1](m)
                s, q = entry_of[2](n)

                @pl.when(jnp.logical_and(entry_of[3], taken(kind, part, s, q)))
                def _():
                    act(kind, n, part)

    def turn_relay(inbox, relay, k):
        def act(kind, n, part):
            at = relay.at[kind, n, part]
            pltpu.make_async_copy(at, at, relay_recv.at[k, kind, n, part]).wait()
            onward_copy(inbox, relay, k, kind, n, part).start()

        slots_do(act)

    def turn_wait_recv(src, inbox, k, q):
        for part in range(PARTS):
            local_copy(src, inbox, k, q, part).wait()

    def turn_wait_send(src, inbox, relay, k):
        for q in range(NQ):
            for part in range(PARTS):

                @pl.when(jnp.logical_not(is_self(q)))
                def _():
                    direct_copy(src, inbox, k, q, part).wait_send()

        def act(kind, n, part):
            onward_copy(inbox, relay, k, kind, n, part).wait_send()

        slots_do(act)

    def swap_matrices():
        n = PHASES * 8
        x, y = iota2((n, n), 0), iota2((n, n), 1)
        flipped = (x // PHASES) * PHASES + (x % STEP) * STEP + (x // STEP) % STEP
        phase = jnp.where(y == flipped, 1.0, 0.0).astype(BF16)
        m = 2 * L
        x, y = iota2((m, m), 0), iota2((m, m), 1)
        flipped = ((x // C) % 2) * L + (x // L) * C + x % C
        lanes = jnp.where(y == flipped, 1.0, 0.0).astype(BF16)
        return phase, lanes

    def turned(inbox, q, phase, lanes):
        got = inbox[q].reshape(nP, 2, nP, PHASES, L)
        pair = jnp.concatenate([got[:, 0], got[:, 1]], axis=-1).reshape(nP * nP * PHASES, 2 * L)
        swapped = dot(pair, lanes).astype(BF16)
        n = phase.shape[0]
        parts = [
            dot(phase, swapped[i * n : (i + 1) * n]).astype(BF16)
            for i in range(nP * nP * PHASES // n)
        ]
        return jnp.concatenate(parts, axis=0).reshape(nP, nP, PHASES, 2 * L)

    pieces = [(-1, 0, 0), (-1, -1, 0), (-1, 1, 0), (1, 0, 0), (1, -1, 0), (1, 1, 0)]
    pieces += [(0, dc, part) for part in range(2) for dc in (-1, 1)]

    def halo_copy(img, k, n):
        dr, dc, part = pieces[n]
        half = nI // 2
        rows = {-1: (2, nI + 2, 2), 0: (2 + part * half,) * 2 + (half,), 1: (nI, 0, 2)}[dr]
        cols = {-1: (1, nP + 1, 1), 0: (1, 1, nP), 1: (nP, 0, 1)}[dc]
        return pltpu.make_async_remote_copy(
            src_ref=img.at[pl.ds(rows[0], rows[2]), pl.ds(cols[0], cols[2])],
            dst_ref=img.at[pl.ds(rows[1], rows[2]), pl.ds(cols[1], cols[2])],
            send_sem=halo_send.at[k, n],
            recv_sem=halo_recv.at[k, n],
            device_id=(r + dr, c + dc),
            device_id_type=MESH,
        )

    def halo_start(img, k, q):
        last = {0: (0, 1, 2), NQ // 2 - 1: (6, 7), NQ - 1: (8, 9, 3, 4, 5)}
        for n in last.get(q, ()):

            @pl.when(exists(pieces[n][:2]))
            def _():
                halo_copy(img, k, n).start()

    def halo_wait(img, k):
        for n, (dr, dc, _) in enumerate(pieces):

            @pl.when(exists((-dr, -dc)))
            def _():
                halo_copy(img, k, n).wait_recv()

            @pl.when(exists((dr, dc)))
            def _():
                halo_copy(img, k, n).wait_send()

    def conv(src, k0, count, p0, pairs, which):
        taps = []
        for dy in range(3):
            got = src[pl.ds(k0 + dy, count), p0 : p0 + pairs + 1]
            for side in range(2):
                taps.append(got[:, side : side + pairs].reshape(count * pairs * PHASES, L))
        return dot(jnp.concatenate(taps, axis=1), packed[which])

    inside = [(2 + t * (nI - 2) // 2, (nI - 2) // 2, 1, nP - 1) for t in range(2)]
    around = [(0, 2, 0, nP + 1), (nI, 2, 0, nP + 1), (2, nI - 2, 0, 1), (2, nI - 2, nP, 1)]

    def clear_outside(img):
        @pl.when(r == 0)
        def _():
            img[0] = jnp.zeros((nP + 1, PHASES, L), BF16)

        @pl.when(r == rows_axis - 1)
        def _():
            img[nI + 1] = jnp.zeros((nP + 1, PHASES, L), BF16)

        @pl.when(c == 0)
        def _():
            img[:, 0, :, 0:C] = jnp.zeros((nI + 2, PHASES, C), BF16)

        @pl.when(c == cols_axis - 1)
        def _():
            img[:, nP, :, C:L] = jnp.zeros((nI + 2, PHASES, C), BF16)

    loads[0].wait()
    enter(feature, own)
    pl.semaphore_wait(barrier, expected)
    turn_start(own, inbox1, relay1, 0, range(NQ))
    turn_relay(inbox1, relay1, 0)

    for load in loads[1:]:
        load.wait()
    enter(cotangent, cot)
    eye = jnp.where(iota2((C, C), 0) == iota2((C, C), 1), 1.0, 0.0).astype(BF16)
    nothing = jnp.zeros((C, C), BF16)
    for which, w, back in ((0, w_first, 0), (1, w_second, 0), (2, w_second, 1), (3, w_first, 1)):
        for dy in range(3):
            tap = [
                dot(eye, w[2 - dy, 2 - kx], NT).astype(BF16) if back else w[dy, kx]
                for kx in range(3)
            ]
            for a in range(4):
                left = tap[a] if a < 3 else nothing
                right = tap[a - 1] if a > 0 else nothing
                packed[which, pl.ds(dy * 4 * C + a * C, C)] = jnp.concatenate([left, right], axis=1)
    bias1 = jnp.concatenate([b_first[...], b_first[...]], axis=1)
    bias2 = jnp.concatenate([b_second[...], b_second[...]], axis=1)

    phase, lanes = swap_matrices()
    for q in range(NQ):
        turn_wait_recv(own, inbox1, 0, q)
        got = turned(inbox1, q, phase, lanes)
        for jp in range(nP):
            for b in range(2):
                i = q * QB + 2 * jp + b
                total = own[i].astype(F32) + got[:, jp, :, b * L : (b + 1) * L].astype(F32)
                sym[i + 2, 1 : nP + 1] = total.astype(BF16)
        halo_start(sym, 0, q)

    def first_layer(k0, count, p0, pairs):
        pre = conv(sym, k0, count, p0, pairs, 0) + bias1
        value, rise = gelu_and_slope(pre)
        size = (count, pairs, PHASES, L)
        hid[pl.ds(k0, count), p0 : p0 + pairs] = value.astype(BF16).reshape(size)
        slope[pl.ds(k0, count), p0 : p0 + pairs] = rise.reshape(size)

    for box in inside:
        first_layer(*box)
    turn_wait_send(own, inbox1, relay1, 0)
    halo_wait(sym, 0)
    for box in around:
        first_layer(*box)
    clear_outside(hid)

    for q in range(NQ):
        k0 = q * QB
        pre = conv(hid, k0, QB, 0, nP, 1) + bias2
        value, rise = gelu_and_slope(pre)
        size = (QB, nP, PHASES, L)
        base = sym[pl.ds(k0 + 2, QB), 1 : nP + 1].astype(F32)
        fresh[pl.ds(k0, QB)] = (base + value.reshape(size)).astype(BF16)
        pull = cot[pl.ds(k0, QB)].astype(F32) * rise.reshape(size)
        g2[pl.ds(k0 + 2, QB), 1 : nP + 1] = pull.astype(BF16)
        halo_start(g2, 1, q)

    def first_pull(k0, count, p0, pairs):
        size = (count, pairs, PHASES, L)
        pulled = conv(g2, k0, count, p0, pairs, 2).reshape(size)
        rise = slope[pl.ds(k0, count), p0 : p0 + pairs]
        g1[pl.ds(k0, count), p0 : p0 + pairs] = (pulled * rise).astype(BF16)

    for box in inside:
        first_pull(*box)
    leave(fresh, out_ref)
    halo_wait(g2, 1)
    for box in around:
        first_pull(*box)

    clear_outside(g1)

    for q in range(NQ):
        k0 = q * QB
        total = conv(g1, k0, QB, 0, nP, 3).reshape(QB, nP, PHASES, L)
        gsym[pl.ds(k0, QB)] = (cot[pl.ds(k0, QB)].astype(F32) + total).astype(BF16)
        turn_start(gsym, inbox2, relay2, 1, [q])
    turn_relay(inbox2, relay2, 1)

    for q in range(NQ):
        turn_wait_recv(gsym, inbox2, 1, q)
        got = turned(inbox2, q, phase, lanes)
        for jp in range(nP):
            for b in range(2):
                i = q * QB + 2 * jp + b
                total = gsym[i].astype(F32) + got[:, jp, :, b * L : (b + 1) * L].astype(F32)
                fresh[i] = total.astype(BF16)
    turn_wait_send(gsym, inbox2, relay2, 1)
    leave(fresh, grad_ref)


def per_device(rows_axis, cols_axis, feature, w1, b1, w2, b2, cotangent):
    TR, TC, C = feature.shape
    nI, nP = TR // STEP, TC // (2 * STEP)
    QB, NQ, L = TC // STEP, TR // TC, 2 * C
    turned = lambda x: jnp.transpose(x, (1, 2, 0))
    image = lambda i, p: pltpu.VMEM((i, p, PHASES, L), BF16)
    vmem = pl.BlockSpec(memory_space=pltpu.VMEM)
    out = jax.ShapeDtypeStruct((TC, C, TR), BF16)
    res = pl.pallas_call(
        functools.partial(kernel, rows_axis, cols_axis),
        out_shape=(out, out),
        in_specs=[pl.BlockSpec(memory_space=pltpu.HBM)] * 6,
        out_specs=(vmem, vmem),
        scratch_shapes=[
            pltpu.VMEM((TC, C, TR), BF16),
            pltpu.VMEM(w1.shape, BF16),
            pltpu.VMEM((1, C), F32),
            pltpu.VMEM(w2.shape, BF16),
            pltpu.VMEM((1, C), F32),
            pltpu.VMEM((TC, C, TR), BF16),
            pltpu.SemaphoreType.DMA((6,)),
            pltpu.VMEM((nI * PHASES, STEP * TR), BF16),
            image(nI, nP),
            image(nI, nP),
            image(nI + 4, nP + 2),
            image(nI + 2, nP + 1),
            image(nI + 4, nP + 2),
            image(nI + 2, nP + 1),
            image(nI, nP),
            image(nI, nP),
            pltpu.VMEM((nI + 2, nP + 1, PHASES, L), F32),
            pltpu.VMEM((4, 12 * C, L), BF16),
            pltpu.VMEM((NQ, QB, nP, PHASES, L), BF16),
            pltpu.VMEM((NQ, QB, nP, PHASES, L), BF16),
            pltpu.VMEM((len(ROUTES), SLOTS, PARTS, QB // PARTS, nP, PHASES, L), BF16),
            pltpu.VMEM((len(ROUTES), SLOTS, PARTS, QB // PARTS, nP, PHASES, L), BF16),
            pltpu.SemaphoreType.DMA((2, 10)),
            pltpu.SemaphoreType.DMA((2, 10)),
            pltpu.SemaphoreType.DMA((2, NQ, PARTS)),
            pltpu.SemaphoreType.DMA((2, NQ, PARTS)),
            pltpu.SemaphoreType.DMA((2, len(ROUTES), SLOTS, PARTS)),
            pltpu.SemaphoreType.DMA((2, len(ROUTES), SLOTS, PARTS)),
        ],
        compiler_params=pltpu.CompilerParams(
            collective_id=0, has_side_effects=True, vmem_limit_bytes=30000000
        ),
    )(
        *(
            pltpu.with_memory_space_constraint(x, pltpu.HBM)
            for x in (
                turned(feature),
                w1,
                b1.reshape(1, C),
                w2,
                b2.reshape(1, C),
                turned(cotangent),
            )
        )
    )
    return tuple(jnp.transpose(x, (2, 0, 1)) for x in res)


def solution(mesh):
    specs = P("row", "col", None)
    return jax.shard_map(
        functools.partial(per_device, mesh.shape["row"], mesh.shape["col"]),
        mesh=mesh,
        in_specs=(specs, P(), P(), P(), P(), specs),
        out_specs=(specs, specs),
        check_vma=False,
    )
```

```python
import functools

import jax
import jax.numpy as jnp
from jax import lax
from jax.experimental import pallas as pl
from jax.experimental.pallas import tpu as pltpu
from jax.sharding import PartitionSpec as P

MESH = pl.DeviceIdType.MESH
STEP = 4
PHASES = STEP * STEP
F32 = jnp.float32
BF16 = jnp.bfloat16
ROOT_HALF = 0.7071067811865476
INV_ROOT_TAU = 0.3989422804014327
SLOTS = 16
PARTS = 1
ROUTES = ((-638580491, 548734887),)
DIRECTIONS = [(-1, 0), (1, 0), (0, -1), (0, 1), (-1, -1), (-1, 1), (1, -1), (1, 1)]
NT = (((1,), (1,)), ((), ()))
TN = (((0,), (0,)), ((), ()))


def iota2(shape, dim):
    return lax.broadcasted_iota(jnp.int32, shape, dim)


def dot(a, b, dims=None):
    if dims is None:
        return jnp.dot(a, b, preferred_element_type=F32)
    return lax.dot_general(a, b, dims, preferred_element_type=F32)


def gelu_and_slope(v):
    half_cdf = 0.5 * (1.0 + lax.erf(v * ROOT_HALF))
    return v * half_cdf, half_cdf + v * jnp.exp(-0.5 * v * v) * INV_ROOT_TAU


def gelu_value(v):
    return 0.5 * v * (1.0 + lax.erf(v * ROOT_HALF))


def kernel(
    rows_axis,
    cols_axis,
    feature_hbm,
    w_first_hbm,
    b_first_hbm,
    w_second_hbm,
    b_second_hbm,
    cotangent_hbm,
    out_ref,
    grad_ref,
    feature,
    w_first,
    b_first,
    w_second,
    b_second,
    cotangent,
    load_sem,
    entry,
    own,
    cot,
    sym,
    hid,
    g2,
    g1,
    gsym,
    fresh,
    slope,
    packed,
    inbox1,
    inbox2,
    relay1,
    relay2,
    halo_send,
    halo_recv,
    turn_send,
    turn_recv,
    relay_send,
    relay_recv,
):
    C = w_first.shape[-1]
    TC, _, TR = feature.shape
    nI, nP = TR // STEP, TC // (2 * STEP)
    QB = TC // STEP
    NQ = TR // TC
    L = 2 * C
    r, c = lax.axis_index("row"), lax.axis_index("col")

    def partner(q):
        return (c // NQ, r * NQ + q)

    def is_self(q):
        return jnp.logical_and(c // NQ == r, r * NQ + q == c)

    def same(a, b):
        return jnp.logical_and(a[0] == b[0], a[1] == b[1])

    me = (r, c)

    def via_xy(s, q):
        return ((s[0] // 4) * 4 + (s[1] // 4) % 4, (s[0] // 2) * 8 + s[1] % 8)

    def via_xy_slot(q):
        return ((c // 16) * 2 + r % 2) * 4 + q

    def via_xy_source(n):
        x = 2 * (n // 8) + (r % 4) // 2
        y = 2 * ((c // 8) % 2) + (n // 4) % 2
        return ((r // 4) * 4 + y, x * 8 + c % 8), n % 4

    kinds = [
        (
            via_xy,
            via_xy_slot,
            via_xy_source,
            jnp.logical_and(r // 4 == c // 16, (c % 8) // 4 == r % 2),
            [((c // 16) * 4 + r % 4, (c // 8) * 8 + (r % 2) * 4 + k) for k in range(4)],
            [via_xy_source(n)[0] for n in range(0, SLOTS, 4)],
            [via_xy(me, 0)],
            16,
            lambda m: ((m % 4) * 4 + m // (4 * PARTS), (m // 4) % PARTS),
        ),
    ]

    def taken(kind, part, s, q):
        x1, x0, y1, y0 = s[1] // 16, (s[1] // 8) % 2, (s[0] % 4) // 2, s[0] % 2
        z2, z1, z0, q1 = (s[1] % 8) // 4, (s[1] // 2) % 2, s[0] // 4, q // 2
        differ = lambda a, b: (a + b) % 2
        at = z1 + 2 * q1 + 4 * differ(x1, z0) + 8 * differ(x0, y1) + 16 * differ(y0, z2)
        words = [jnp.int32(word) for word in ROUTES[kind]]
        word = words[q % 2] if isinstance(q, int) else jnp.where(q % 2 == 0, *words)
        w = kinds[kind][0](s, q)
        target = (s[1] // NQ, s[0] * NQ + q)
        aside = jnp.logical_not(jnp.logical_or(same(w, s), same(w, target)))
        return jnp.logical_and(aside, lax.shift_right_logical(word, at) % 2 == 1)

    def exists(d):
        dr, dc = d
        ok = None
        for delta, pos, size in ((dr, r, rows_axis), (dc, c, cols_axis)):
            if delta == -1:
                cond = pos > 0
            elif delta == 1:
                cond = pos < size - 1
            else:
                continue
            ok = cond if ok is None else jnp.logical_and(ok, cond)
        return ok

    loads = [
        pltpu.make_async_copy(a, b, load_sem.at[i])
        for i, (a, b) in enumerate(
            (
                (feature_hbm, feature),
                (cotangent_hbm, cotangent),
                (w_first_hbm, w_first),
                (w_second_hbm, w_second),
                (b_first_hbm, b_first),
                (b_second_hbm, b_second),
            )
        )
    ]
    for load in loads:
        load.start()

    for img in (sym, g2):
        img[0:2] = jnp.zeros((2, nP + 2, PHASES, L), BF16)
        img[nI + 2 : nI + 4] = jnp.zeros((2, nP + 2, PHASES, L), BF16)
        img[:, 0:1] = jnp.zeros((nI + 4, 1, PHASES, L), BF16)
        img[:, nP + 1 : nP + 2] = jnp.zeros((nI + 4, 1, PHASES, L), BF16)

    barrier = pltpu.get_barrier_semaphore()
    expected = jnp.int32(0)
    for q in range(NQ):
        other = jnp.logical_not(is_self(q))
        expected = expected + other.astype(jnp.int32)

        @pl.when(other)
        def _():
            pl.semaphore_signal(barrier, inc=1, device_id=partner(q), device_id_type=MESH)

    def greet(other):
        @pl.when(jnp.logical_not(same(other, me)))
        def _():
            pl.semaphore_signal(barrier, inc=1, device_id=other, device_id_type=MESH)

    for _, _, _, relaying, relays, sources, firsts, targets, _ in kinds:
        greeted = jnp.int32(targets)
        for other in relays:
            greet(other)
            greeted = greeted - same(other, me).astype(jnp.int32)
        for other in firsts:
            expected = expected + jnp.logical_not(same(other, me)).astype(jnp.int32)
        expected = expected + jnp.where(relaying, greeted, 0)

        @pl.when(relaying)
        def _():
            for other in sources:
                greet(other)

    for d in DIRECTIONS:
        here = exists(d)
        expected = expected + here.astype(jnp.int32)

        @pl.when(here)
        def _():
            pl.semaphore_signal(
                barrier, inc=1, device_id=(r + d[0], c + d[1]), device_id_type=MESH
            )

    shape = (nI * PHASES, STEP * TR)
    at = iota2(shape, 0)
    target = ((at // STEP) % STEP) * TR + (at // PHASES) * STEP + at % STEP
    entry[...] = jnp.where(iota2(shape, 1) == target, 1.0, 0.0).astype(BF16)

    def enter(src, dst):
        for jp in range(nP):
            base = jp * 2 * STEP
            blocks = [
                jnp.concatenate([src[base + s], src[base + STEP + s]], axis=0) for s in range(STEP)
            ]
            res = dot(entry[...], jnp.concatenate(blocks, axis=1), NT)
            dst[:, jp] = res.astype(BF16).reshape(nI, PHASES, L)

    def leave(src, dst):
        for jp in range(nP):
            base = jp * 2 * STEP
            res = dot(src[:, jp].reshape(nI * PHASES, L), entry[...], TN).astype(BF16)
            for b in range(2):
                for s in range(STEP):
                    dst[base + STEP * b + s] = res[b * C : (b + 1) * C, s * TR : (s + 1) * TR]

    half_rows = QB // PARTS

    def part_rows(part):
        return pl.ds(part * half_rows, half_rows)

    def block(src, q, part):
        return src.at[pl.ds(q * QB + part * half_rows, half_rows)]

    def direct_copy(src, inbox, k, q, part):
        slot = lax.rem(c, NQ)
        return pltpu.make_async_remote_copy(
            src_ref=block(src, q, part),
            dst_ref=inbox.at[slot, part_rows(part)],
            send_sem=turn_send.at[k, q, part],
            recv_sem=turn_recv.at[k, slot, part],
            device_id=partner(q),
            device_id_type=MESH,
        )

    def first_copy(src, relay, k, kind, q, part):
        slot = kinds[kind][1](q)
        return pltpu.make_async_remote_copy(
            src_ref=block(src, q, part),
            dst_ref=relay.at[kind, slot, part],
            send_sem=turn_send.at[k, q, part],
            recv_sem=relay_recv.at[k, kind, slot, part],
            device_id=kinds[kind][0](me, q),
            device_id_type=MESH,
        )

    def onward_copy(inbox, relay, k, kind, n, part):
        s, q = kinds[kind][2](n)
        slot = lax.rem(s[1], NQ)
        return pltpu.make_async_remote_copy(
            src_ref=relay.at[kind, n, part],
            dst_ref=inbox.at[slot, part_rows(part)],
            send_sem=relay_send.at[k, kind, n, part],
            recv_sem=turn_recv.at[k, slot, part],
            device_id=(s[1] // NQ, s[0] * NQ + q),
            device_id_type=MESH,
        )

    def local_copy(src, inbox, k, q, part):
        return pltpu.make_async_copy(
            block(src, q, part), inbox.at[q, part_rows(part)], turn_recv.at[k, q, part]
        )

    def way(q, part):
        by = [taken(kind, part, me, q) for kind in range(len(kinds))]
        straight = jnp.logical_not(is_self(q))
        for one in by:
            straight = jnp.logical_and(straight, jnp.logical_not(one))
        return by, straight

    ways = {(q, part): way(q, part) for q in range(NQ) for part in range(PARTS)}

    def turn_start(src, inbox, relay, k, qs):
        for q in qs:
            for part in range(PARTS):
                for kind, one in enumerate(ways[q, part][0]):

                    @pl.when(one)
                    def _():
                        first_copy(src, relay, k, kind, q, part).start()

        for q in qs:
            for part in range(PARTS):

                @pl.when(ways[q, part][1])
                def _():
                    direct_copy(src, inbox, k, q, part).start()

            @pl.when(is_self(q))
            def _():
                for part in range(PARTS):
                    local_copy(src, inbox, k, q, part).start()

    def slots_do(act):
        @pl.loop(0, PARTS * SLOTS)
        def _(m):
            for kind, entry_of in enumerate(kinds):
                n, part = entry_of[-1](m)
                s, q = entry_of[2](n)

                @pl.when(jnp.logical_and(entry_of[3], taken(kind, part, s, q)))
                def _():
                    act(kind, n, part)

    def turn_relay(inbox, relay, k):
        def act(kind, n, part):
            at = relay.at[kind, n, part]
            pltpu.make_async_copy(at, at, relay_recv.at[k, kind, n, part]).wait()
            onward_copy(inbox, relay, k, kind, n, part).start()

        slots_do(act)

    def turn_wait_recv(src, inbox, k, q):
        for part in range(PARTS):
            local_copy(src, inbox, k, q, part).wait()

    def turn_wait_send(src, inbox, relay, k):
        for q in range(NQ):
            for part in range(PARTS):

                @pl.when(jnp.logical_not(is_self(q)))
                def _():
                    direct_copy(src, inbox, k, q, part).wait_send()

        def act(kind, n, part):
            onward_copy(inbox, relay, k, kind, n, part).wait_send()

        slots_do(act)

    def swap_matrices():
        n = PHASES * 8
        x, y = iota2((n, n), 0), iota2((n, n), 1)
        flipped = (x // PHASES) * PHASES + (x % STEP) * STEP + (x // STEP) % STEP
        phase = jnp.where(y == flipped, 1.0, 0.0).astype(BF16)
        m = 2 * L
        x, y = iota2((m, m), 0), iota2((m, m), 1)
        flipped = ((x // C) % 2) * L + (x // L) * C + x % C
        lanes = jnp.where(y == flipped, 1.0, 0.0).astype(BF16)
        return phase, lanes

    def turned(inbox, q, phase, lanes):
        got = inbox[q].reshape(nP, 2, nP, PHASES, L)
        pair = jnp.concatenate([got[:, 0], got[:, 1]], axis=-1).reshape(nP * nP * PHASES, 2 * L)
        swapped = dot(pair, lanes).astype(BF16)
        n = phase.shape[0]
        parts = [
            dot(phase, swapped[i * n : (i + 1) * n]).astype(BF16)
            for i in range(nP * nP * PHASES // n)
        ]
        return jnp.concatenate(parts, axis=0).reshape(nP, nP, PHASES, 2 * L)

    pieces = [(-1, 0, 0), (-1, -1, 0), (-1, 1, 0), (1, 0, 0), (1, -1, 0), (1, 1, 0)]
    pieces += [(0, dc, part) for part in range(2) for dc in (-1, 1)]

    def halo_copy(img, k, n):
        dr, dc, part = pieces[n]
        half = nI // 2
        rows = {-1: (2, nI + 2, 2), 0: (2 + part * half,) * 2 + (half,), 1: (nI, 0, 2)}[dr]
        cols = {-1: (1, nP + 1, 1), 0: (1, 1, nP), 1: (nP, 0, 1)}[dc]
        return pltpu.make_async_remote_copy(
            src_ref=img.at[pl.ds(rows[0], rows[2]), pl.ds(cols[0], cols[2])],
            dst_ref=img.at[pl.ds(rows[1], rows[2]), pl.ds(cols[1], cols[2])],
            send_sem=halo_send.at[k, n],
            recv_sem=halo_recv.at[k, n],
            device_id=(r + dr, c + dc),
            device_id_type=MESH,
        )

    def halo_start(img, k, q):
        last = {0: (0, 1, 2), NQ // 2 - 1: (6, 7), NQ - 1: (4, 5, 3, 8, 9)}
        for n in last.get(q, ()):

            @pl.when(exists(pieces[n][:2]))
            def _():
                halo_copy(img, k, n).start()

    def halo_wait(img, k):
        for n, (dr, dc, _) in enumerate(pieces):

            @pl.when(exists((-dr, -dc)))
            def _():
                halo_copy(img, k, n).wait_recv()

            @pl.when(exists((dr, dc)))
            def _():
                halo_copy(img, k, n).wait_send()

    def conv(src, k0, count, p0, pairs, which):
        taps = []
        for dy in range(3):
            got = src[pl.ds(k0 + dy, count), p0 : p0 + pairs + 1]
            for side in range(2):
                taps.append(got[:, side : side + pairs].reshape(count * pairs * PHASES, L))
        return dot(jnp.concatenate(taps, axis=1), packed[which])

    inside = [(2 + t * (nI - 2) // 2, (nI - 2) // 2, 1, nP - 1) for t in range(2)]
    around = [(0, 2, 0, nP + 1), (nI, 2, 0, nP + 1), (2, nI - 2, 0, 1), (2, nI - 2, nP, 1)]

    def clear_outside(img):
        @pl.when(r == 0)
        def _():
            img[0] = jnp.zeros((nP + 1, PHASES, L), BF16)

        @pl.when(r == rows_axis - 1)
        def _():
            img[nI + 1] = jnp.zeros((nP + 1, PHASES, L), BF16)

        @pl.when(c == 0)
        def _():
            img[:, 0, :, 0:C] = jnp.zeros((nI + 2, PHASES, C), BF16)

        @pl.when(c == cols_axis - 1)
        def _():
            img[:, nP, :, C:L] = jnp.zeros((nI + 2, PHASES, C), BF16)

    loads[0].wait()
    enter(feature, own)
    pl.semaphore_wait(barrier, expected)
    turn_start(own, inbox1, relay1, 0, range(NQ))
    turn_relay(inbox1, relay1, 0)

    for load in loads[1:]:
        load.wait()
    enter(cotangent, cot)
    eye = jnp.where(iota2((C, C), 0) == iota2((C, C), 1), 1.0, 0.0).astype(BF16)
    nothing = jnp.zeros((C, C), BF16)
    for which, w, back in ((0, w_first, 0), (1, w_second, 0), (2, w_second, 1), (3, w_first, 1)):
        for dy in range(3):
            tap = [
                dot(eye, w[2 - dy, 2 - kx], NT).astype(BF16) if back else w[dy, kx]
                for kx in range(3)
            ]
            for a in range(4):
                left = tap[a] if a < 3 else nothing
                right = tap[a - 1] if a > 0 else nothing
                packed[which, pl.ds(dy * 4 * C + a * C, C)] = jnp.concatenate([left, right], axis=1)
    bias1 = jnp.concatenate([b_first[...], b_first[...]], axis=1)
    bias2 = jnp.concatenate([b_second[...], b_second[...]], axis=1)

    phase, lanes = swap_matrices()
    for q in range(NQ):
        turn_wait_recv(own, inbox1, 0, q)
        got = turned(inbox1, q, phase, lanes)
        for jp in range(nP):
            for b in range(2):
                i = q * QB + 2 * jp + b
                total = own[i].astype(F32) + got[:, jp, :, b * L : (b + 1) * L].astype(F32)
                sym[i + 2, 1 : nP + 1] = total.astype(BF16)
        halo_start(sym, 0, q)

    def first_layer(k0, count, p0, pairs):
        pre = conv(sym, k0, count, p0, pairs, 0) + bias1
        value, rise = gelu_and_slope(pre)
        size = (count, pairs, PHASES, L)
        hid[pl.ds(k0, count), p0 : p0 + pairs] = value.astype(BF16).reshape(size)
        slope[pl.ds(k0, count), p0 : p0 + pairs] = rise.reshape(size)

    for box in inside:
        first_layer(*box)
    turn_wait_send(own, inbox1, relay1, 0)
    halo_wait(sym, 0)
    for box in around:
        first_layer(*box)
    clear_outside(hid)

    for q in range(NQ):
        k0 = q * QB
        pre = conv(hid, k0, QB, 0, nP, 1) + bias2
        value, rise = gelu_and_slope(pre)
        size = (QB, nP, PHASES, L)
        base = sym[pl.ds(k0 + 2, QB), 1 : nP + 1].astype(F32)
        fresh[pl.ds(k0, QB)] = (base + value.reshape(size)).astype(BF16)
        pull = cot[pl.ds(k0, QB)].astype(F32) * rise.reshape(size)
        g2[pl.ds(k0 + 2, QB), 1 : nP + 1] = pull.astype(BF16)
        halo_start(g2, 1, q)

    def first_pull(k0, count, p0, pairs):
        size = (count, pairs, PHASES, L)
        pulled = conv(g2, k0, count, p0, pairs, 2).reshape(size)
        rise = slope[pl.ds(k0, count), p0 : p0 + pairs]
        g1[pl.ds(k0, count), p0 : p0 + pairs] = (pulled * rise).astype(BF16)

    for box in inside:
        first_pull(*box)
    leave(fresh, out_ref)
    halo_wait(g2, 1)
    for box in around:
        first_pull(*box)

    clear_outside(g1)

    for q in range(NQ):
        k0 = q * QB
        total = conv(g1, k0, QB, 0, nP, 3).reshape(QB, nP, PHASES, L)
        gsym[pl.ds(k0, QB)] = (cot[pl.ds(k0, QB)].astype(F32) + total).astype(BF16)
        turn_start(gsym, inbox2, relay2, 1, [q])
    turn_relay(inbox2, relay2, 1)

    for q in range(NQ):
        turn_wait_recv(gsym, inbox2, 1, q)
        got = turned(inbox2, q, phase, lanes)
        for jp in range(nP):
            for b in range(2):
                i = q * QB + 2 * jp + b
                total = gsym[i].astype(F32) + got[:, jp, :, b * L : (b + 1) * L].astype(F32)
                fresh[i] = total.astype(BF16)
    turn_wait_send(gsym, inbox2, relay2, 1)
    leave(fresh, grad_ref)


def per_device(rows_axis, cols_axis, feature, w1, b1, w2, b2, cotangent):
    TR, TC, C = feature.shape
    nI, nP = TR // STEP, TC // (2 * STEP)
    QB, NQ, L = TC // STEP, TR // TC, 2 * C
    turned = lambda x: jnp.transpose(x, (1, 2, 0))
    image = lambda i, p: pltpu.VMEM((i, p, PHASES, L), BF16)
    vmem = pl.BlockSpec(memory_space=pltpu.VMEM)
    out = jax.ShapeDtypeStruct((TC, C, TR), BF16)
    res = pl.pallas_call(
        functools.partial(kernel, rows_axis, cols_axis),
        out_shape=(out, out),
        in_specs=[pl.BlockSpec(memory_space=pltpu.HBM)] * 6,
        out_specs=(vmem, vmem),
        scratch_shapes=[
            pltpu.VMEM((TC, C, TR), BF16),
            pltpu.VMEM(w1.shape, BF16),
            pltpu.VMEM((1, C), F32),
            pltpu.VMEM(w2.shape, BF16),
            pltpu.VMEM((1, C), F32),
            pltpu.VMEM((TC, C, TR), BF16),
            pltpu.SemaphoreType.DMA((6,)),
            pltpu.VMEM((nI * PHASES, STEP * TR), BF16),
            image(nI, nP),
            image(nI, nP),
            image(nI + 4, nP + 2),
            image(nI + 2, nP + 1),
            image(nI + 4, nP + 2),
            image(nI + 2, nP + 1),
            image(nI, nP),
            image(nI, nP),
            pltpu.VMEM((nI + 2, nP + 1, PHASES, L), F32),
            pltpu.VMEM((4, 12 * C, L), BF16),
            pltpu.VMEM((NQ, QB, nP, PHASES, L), BF16),
            pltpu.VMEM((NQ, QB, nP, PHASES, L), BF16),
            pltpu.VMEM((len(ROUTES), SLOTS, PARTS, QB // PARTS, nP, PHASES, L), BF16),
            pltpu.VMEM((len(ROUTES), SLOTS, PARTS, QB // PARTS, nP, PHASES, L), BF16),
            pltpu.SemaphoreType.DMA((2, 10)),
            pltpu.SemaphoreType.DMA((2, 10)),
            pltpu.SemaphoreType.DMA((2, NQ, PARTS)),
            pltpu.SemaphoreType.DMA((2, NQ, PARTS)),
            pltpu.SemaphoreType.DMA((2, len(ROUTES), SLOTS, PARTS)),
            pltpu.SemaphoreType.DMA((2, len(ROUTES), SLOTS, PARTS)),
        ],
        compiler_params=pltpu.CompilerParams(
            collective_id=0, has_side_effects=True, vmem_limit_bytes=30000000
        ),
    )(
        *(
            pltpu.with_memory_space_constraint(x, pltpu.HBM)
            for x in (
                turned(feature),
                w1,
                b1.reshape(1, C),
                w2,
                b2.reshape(1, C),
                turned(cotangent),
            )
        )
    )
    return tuple(jnp.transpose(x, (2, 0, 1)) for x in res)


def solution(mesh):
    specs = P("row", "col", None)
    return jax.shard_map(
        functools.partial(per_device, mesh.shape["row"], mesh.shape["col"]),
        mesh=mesh,
        in_specs=(specs, P(), P(), P(), P(), specs),
        out_specs=(specs, specs),
        check_vma=False,
    )
```

```python
import functools

import jax
import jax.numpy as jnp
from jax import lax
from jax.experimental import pallas as pl
from jax.experimental.pallas import tpu as pltpu
from jax.sharding import PartitionSpec as P

MESH = pl.DeviceIdType.MESH
STEP = 4
PHASES = STEP * STEP
F32 = jnp.float32
BF16 = jnp.bfloat16
ROOT_HALF = 0.7071067811865476
INV_ROOT_TAU = 0.3989422804014327
SLOTS = 16
PARTS = 1
ROUTES = ((-638580491, 548734887),)
DIRECTIONS = [(-1, 0), (1, 0), (0, -1), (0, 1), (-1, -1), (-1, 1), (1, -1), (1, 1)]
NT = (((1,), (1,)), ((), ()))
TN = (((0,), (0,)), ((), ()))


def iota2(shape, dim):
    return lax.broadcasted_iota(jnp.int32, shape, dim)


def dot(a, b, dims=None):
    if dims is None:
        return jnp.dot(a, b, preferred_element_type=F32)
    return lax.dot_general(a, b, dims, preferred_element_type=F32)


def gelu_and_slope(v):
    half_cdf = 0.5 * (1.0 + lax.erf(v * ROOT_HALF))
    return v * half_cdf, half_cdf + v * jnp.exp(-0.5 * v * v) * INV_ROOT_TAU


def gelu_value(v):
    return 0.5 * v * (1.0 + lax.erf(v * ROOT_HALF))


def kernel(
    rows_axis,
    cols_axis,
    feature_hbm,
    w_first_hbm,
    b_first_hbm,
    w_second_hbm,
    b_second_hbm,
    cotangent_hbm,
    out_ref,
    grad_ref,
    feature,
    w_first,
    b_first,
    w_second,
    b_second,
    cotangent,
    load_sem,
    entry,
    own,
    cot,
    sym,
    hid,
    g2,
    g1,
    gsym,
    fresh,
    slope,
    packed,
    inbox1,
    inbox2,
    relay1,
    relay2,
    halo_send,
    halo_recv,
    turn_send,
    turn_recv,
    relay_send,
    relay_recv,
):
    C = w_first.shape[-1]
    TC, _, TR = feature.shape
    nI, nP = TR // STEP, TC // (2 * STEP)
    QB = TC // STEP
    NQ = TR // TC
    L = 2 * C
    r, c = lax.axis_index("row"), lax.axis_index("col")

    def partner(q):
        return (c // NQ, r * NQ + q)

    def is_self(q):
        return jnp.logical_and(c // NQ == r, r * NQ + q == c)

    def same(a, b):
        return jnp.logical_and(a[0] == b[0], a[1] == b[1])

    me = (r, c)

    def via_xy(s, q):
        return ((s[0] // 4) * 4 + (s[1] // 4) % 4, (s[0] // 2) * 8 + s[1] % 8)

    def via_xy_slot(q):
        return ((c // 16) * 2 + r % 2) * 4 + q

    def via_xy_source(n):
        x = 2 * (n // 8) + (r % 4) // 2
        y = 2 * ((c // 8) % 2) + (n // 4) % 2
        return ((r // 4) * 4 + y, x * 8 + c % 8), n % 4

    kinds = [
        (
            via_xy,
            via_xy_slot,
            via_xy_source,
            jnp.logical_and(r // 4 == c // 16, (c % 8) // 4 == r % 2),
            [((c // 16) * 4 + r % 4, (c // 8) * 8 + (r % 2) * 4 + k) for k in range(4)],
            [via_xy_source(n)[0] for n in range(0, SLOTS, 4)],
            [via_xy(me, 0)],
            16,
            lambda m: ((m % 4) * 4 + m // (4 * PARTS), (m // 4) % PARTS),
        ),
    ]

    def taken(kind, part, s, q):
        x1, x0, y1, y0 = s[1] // 16, (s[1] // 8) % 2, (s[0] % 4) // 2, s[0] % 2
        z2, z1, z0, q1 = (s[1] % 8) // 4, (s[1] // 2) % 2, s[0] // 4, q // 2
        differ = lambda a, b: (a + b) % 2
        at = z1 + 2 * q1 + 4 * differ(x1, z0) + 8 * differ(x0, y1) + 16 * differ(y0, z2)
        words = [jnp.int32(word) for word in ROUTES[kind]]
        word = words[q % 2] if isinstance(q, int) else jnp.where(q % 2 == 0, *words)
        w = kinds[kind][0](s, q)
        target = (s[1] // NQ, s[0] * NQ + q)
        aside = jnp.logical_not(jnp.logical_or(same(w, s), same(w, target)))
        return jnp.logical_and(aside, lax.shift_right_logical(word, at) % 2 == 1)

    def exists(d):
        dr, dc = d
        ok = None
        for delta, pos, size in ((dr, r, rows_axis), (dc, c, cols_axis)):
            if delta == -1:
                cond = pos > 0
            elif delta == 1:
                cond = pos < size - 1
            else:
                continue
            ok = cond if ok is None else jnp.logical_and(ok, cond)
        return ok

    loads = [
        pltpu.make_async_copy(a, b, load_sem.at[i])
        for i, (a, b) in enumerate(
            (
                (feature_hbm, feature),
                (cotangent_hbm, cotangent),
                (w_first_hbm, w_first),
                (w_second_hbm, w_second),
                (b_first_hbm, b_first),
                (b_second_hbm, b_second),
            )
        )
    ]
    for load in loads:
        load.start()

    for img in (sym, g2):
        img[0:2] = jnp.zeros((2, nP + 2, PHASES, L), BF16)
        img[nI + 2 : nI + 4] = jnp.zeros((2, nP + 2, PHASES, L), BF16)
        img[:, 0:1] = jnp.zeros((nI + 4, 1, PHASES, L), BF16)
        img[:, nP + 1 : nP + 2] = jnp.zeros((nI + 4, 1, PHASES, L), BF16)

    barrier = pltpu.get_barrier_semaphore()
    expected = jnp.int32(0)
    for q in range(NQ):
        other = jnp.logical_not(is_self(q))
        expected = expected + other.astype(jnp.int32)

        @pl.when(other)
        def _():
            pl.semaphore_signal(barrier, inc=1, device_id=partner(q), device_id_type=MESH)

    def greet(other):
        @pl.when(jnp.logical_not(same(other, me)))
        def _():
            pl.semaphore_signal(barrier, inc=1, device_id=other, device_id_type=MESH)

    for _, _, _, relaying, relays, sources, firsts, targets, _ in kinds:
        greeted = jnp.int32(targets)
        for other in relays:
            greet(other)
            greeted = greeted - same(other, me).astype(jnp.int32)
        for other in firsts:
            expected = expected + jnp.logical_not(same(other, me)).astype(jnp.int32)
        expected = expected + jnp.where(relaying, greeted, 0)

        @pl.when(relaying)
        def _():
            for other in sources:
                greet(other)

    for d in DIRECTIONS:
        here = exists(d)
        expected = expected + here.astype(jnp.int32)

        @pl.when(here)
        def _():
            pl.semaphore_signal(
                barrier, inc=1, device_id=(r + d[0], c + d[1]), device_id_type=MESH
            )

    shape = (nI * PHASES, STEP * TR)
    at = iota2(shape, 0)
    target = ((at // STEP) % STEP) * TR + (at // PHASES) * STEP + at % STEP
    entry[...] = jnp.where(iota2(shape, 1) == target, 1.0, 0.0).astype(BF16)

    def enter(src, dst):
        for jp in range(nP):
            base = jp * 2 * STEP
            blocks = [
                jnp.concatenate([src[base + s], src[base + STEP + s]], axis=0) for s in range(STEP)
            ]
            res = dot(entry[...], jnp.concatenate(blocks, axis=1), NT)
            dst[:, jp] = res.astype(BF16).reshape(nI, PHASES, L)

    def leave(src, dst):
        for jp in range(nP):
            base = jp * 2 * STEP
            res = dot(src[:, jp].reshape(nI * PHASES, L), entry[...], TN).astype(BF16)
            for b in range(2):
                for s in range(STEP):
                    dst[base + STEP * b + s] = res[b * C : (b + 1) * C, s * TR : (s + 1) * TR]

    half_rows = QB // PARTS

    def part_rows(part):
        return pl.ds(part * half_rows, half_rows)

    def block(src, q, part):
        return src.at[pl.ds(q * QB + part * half_rows, half_rows)]

    def direct_copy(src, inbox, k, q, part):
        slot = lax.rem(c, NQ)
        return pltpu.make_async_remote_copy(
            src_ref=block(src, q, part),
            dst_ref=inbox.at[slot, part_rows(part)],
            send_sem=turn_send.at[k, q, part],
            recv_sem=turn_recv.at[k, slot, part],
            device_id=partner(q),
            device_id_type=MESH,
        )

    def first_copy(src, relay, k, kind, q, part):
        slot = kinds[kind][1](q)
        return pltpu.make_async_remote_copy(
            src_ref=block(src, q, part),
            dst_ref=relay.at[kind, slot, part],
            send_sem=turn_send.at[k, q, part],
            recv_sem=relay_recv.at[k, kind, slot, part],
            device_id=kinds[kind][0](me, q),
            device_id_type=MESH,
        )

    def onward_copy(inbox, relay, k, kind, n, part):
        s, q = kinds[kind][2](n)
        slot = lax.rem(s[1], NQ)
        return pltpu.make_async_remote_copy(
            src_ref=relay.at[kind, n, part],
            dst_ref=inbox.at[slot, part_rows(part)],
            send_sem=relay_send.at[k, kind, n, part],
            recv_sem=turn_recv.at[k, slot, part],
            device_id=(s[1] // NQ, s[0] * NQ + q),
            device_id_type=MESH,
        )

    def local_copy(src, inbox, k, q, part):
        return pltpu.make_async_copy(
            block(src, q, part), inbox.at[q, part_rows(part)], turn_recv.at[k, q, part]
        )

    def way(q, part):
        by = [taken(kind, part, me, q) for kind in range(len(kinds))]
        straight = jnp.logical_not(is_self(q))
        for one in by:
            straight = jnp.logical_and(straight, jnp.logical_not(one))
        return by, straight

    ways = {(q, part): way(q, part) for q in range(NQ) for part in range(PARTS)}

    def turn_start(src, inbox, relay, k, qs):
        for q in qs:
            for part in range(PARTS):
                for kind, one in enumerate(ways[q, part][0]):

                    @pl.when(one)
                    def _():
                        first_copy(src, relay, k, kind, q, part).start()

        for q in qs:
            for part in range(PARTS):

                @pl.when(ways[q, part][1])
                def _():
                    direct_copy(src, inbox, k, q, part).start()

            @pl.when(is_self(q))
            def _():
                for part in range(PARTS):
                    local_copy(src, inbox, k, q, part).start()

    def slots_do(act):
        @pl.loop(0, PARTS * SLOTS)
        def _(m):
            for kind, entry_of in enumerate(kinds):
                n, part = entry_of[-1](m)
                s, q = entry_of[2](n)

                @pl.when(jnp.logical_and(entry_of[3], taken(kind, part, s, q)))
                def _():
                    act(kind, n, part)

    def turn_relay(inbox, relay, k):
        def act(kind, n, part):
            at = relay.at[kind, n, part]
            pltpu.make_async_copy(at, at, relay_recv.at[k, kind, n, part]).wait()
            onward_copy(inbox, relay, k, kind, n, part).start()

        slots_do(act)

    def turn_wait_recv(src, inbox, k, q):
        for part in range(PARTS):
            local_copy(src, inbox, k, q, part).wait()

    def turn_wait_send(src, inbox, relay, k):
        for q in range(NQ):
            for part in range(PARTS):

                @pl.when(jnp.logical_not(is_self(q)))
                def _():
                    direct_copy(src, inbox, k, q, part).wait_send()

        def act(kind, n, part):
            onward_copy(inbox, relay, k, kind, n, part).wait_send()

        slots_do(act)

    def swap_matrices():
        n = PHASES * 8
        x, y = iota2((n, n), 0), iota2((n, n), 1)
        flipped = (x // PHASES) * PHASES + (x % STEP) * STEP + (x // STEP) % STEP
        phase = jnp.where(y == flipped, 1.0, 0.0).astype(BF16)
        m = 2 * L
        x, y = iota2((m, m), 0), iota2((m, m), 1)
        flipped = ((x // C) % 2) * L + (x // L) * C + x % C
        lanes = jnp.where(y == flipped, 1.0, 0.0).astype(BF16)
        return phase, lanes

    def turned(inbox, q, phase, lanes):
        got = inbox[q].reshape(nP, 2, nP, PHASES, L)
        pair = jnp.concatenate([got[:, 0], got[:, 1]], axis=-1).reshape(nP * nP * PHASES, 2 * L)
        swapped = dot(pair, lanes).astype(BF16)
        n = phase.shape[0]
        parts = [
            dot(phase, swapped[i * n : (i + 1) * n]).astype(BF16)
            for i in range(nP * nP * PHASES // n)
        ]
        return jnp.concatenate(parts, axis=0).reshape(nP, nP, PHASES, 2 * L)

    pieces = [(-1, 0, 0), (-1, -1, 0), (-1, 1, 0), (1, 0, 0), (1, -1, 0), (1, 1, 0)]
    pieces += [(0, dc, part) for part in range(2) for dc in (-1, 1)]

    def halo_copy(img, k, n):
        dr, dc, part = pieces[n]
        half = nI // 2
        rows = {-1: (2, nI + 2, 2), 0: (2 + part * half,) * 2 + (half,), 1: (nI, 0, 2)}[dr]
        cols = {-1: (1, nP + 1, 1), 0: (1, 1, nP), 1: (nP, 0, 1)}[dc]
        return pltpu.make_async_remote_copy(
            src_ref=img.at[pl.ds(rows[0], rows[2]), pl.ds(cols[0], cols[2])],
            dst_ref=img.at[pl.ds(rows[1], rows[2]), pl.ds(cols[1], cols[2])],
            send_sem=halo_send.at[k, n],
            recv_sem=halo_recv.at[k, n],
            device_id=(r + dr, c + dc),
            device_id_type=MESH,
        )

    def halo_start(img, k, q):
        last = {0: (1, 2, 0), NQ // 2 - 1: (6, 7), NQ - 1: (4, 5, 3, 8, 9)}
        for n in last.get(q, ()):

            @pl.when(exists(pieces[n][:2]))
            def _():
                halo_copy(img, k, n).start()

    def halo_wait(img, k):
        for n, (dr, dc, _) in enumerate(pieces):

            @pl.when(exists((-dr, -dc)))
            def _():
                halo_copy(img, k, n).wait_recv()

            @pl.when(exists((dr, dc)))
            def _():
                halo_copy(img, k, n).wait_send()

    def conv(src, k0, count, p0, pairs, which):
        taps = []
        for dy in range(3):
            got = src[pl.ds(k0 + dy, count), p0 : p0 + pairs + 1]
            for side in range(2):
                taps.append(got[:, side : side + pairs].reshape(count * pairs * PHASES, L))
        return dot(jnp.concatenate(taps, axis=1), packed[which])

    inside = [(2 + t * (nI - 2) // 2, (nI - 2) // 2, 1, nP - 1) for t in range(2)]
    around = [(0, 2, 0, nP + 1), (nI, 2, 0, nP + 1), (2, nI - 2, 0, 1), (2, nI - 2, nP, 1)]

    def clear_outside(img):
        @pl.when(r == 0)
        def _():
            img[0] = jnp.zeros((nP + 1, PHASES, L), BF16)

        @pl.when(r == rows_axis - 1)
        def _():
            img[nI + 1] = jnp.zeros((nP + 1, PHASES, L), BF16)

        @pl.when(c == 0)
        def _():
            img[:, 0, :, 0:C] = jnp.zeros((nI + 2, PHASES, C), BF16)

        @pl.when(c == cols_axis - 1)
        def _():
            img[:, nP, :, C:L] = jnp.zeros((nI + 2, PHASES, C), BF16)

    loads[0].wait()
    enter(feature, own)
    pl.semaphore_wait(barrier, expected)
    turn_start(own, inbox1, relay1, 0, range(NQ))
    turn_relay(inbox1, relay1, 0)

    for load in loads[1:]:
        load.wait()
    enter(cotangent, cot)
    eye = jnp.where(iota2((C, C), 0) == iota2((C, C), 1), 1.0, 0.0).astype(BF16)
    nothing = jnp.zeros((C, C), BF16)
    for which, w, back in ((0, w_first, 0), (1, w_second, 0), (2, w_second, 1), (3, w_first, 1)):
        for dy in range(3):
            tap = [
                dot(eye, w[2 - dy, 2 - kx], NT).astype(BF16) if back else w[dy, kx]
                for kx in range(3)
            ]
            for a in range(4):
                left = tap[a] if a < 3 else nothing
                right = tap[a - 1] if a > 0 else nothing
                packed[which, pl.ds(dy * 4 * C + a * C, C)] = jnp.concatenate([left, right], axis=1)
    bias1 = jnp.concatenate([b_first[...], b_first[...]], axis=1)
    bias2 = jnp.concatenate([b_second[...], b_second[...]], axis=1)

    phase, lanes = swap_matrices()
    for q in range(NQ):
        turn_wait_recv(own, inbox1, 0, q)
        got = turned(inbox1, q, phase, lanes)
        for jp in range(nP):
            for b in range(2):
                i = q * QB + 2 * jp + b
                total = own[i].astype(F32) + got[:, jp, :, b * L : (b + 1) * L].astype(F32)
                sym[i + 2, 1 : nP + 1] = total.astype(BF16)
        halo_start(sym, 0, q)

    def first_layer(k0, count, p0, pairs):
        pre = conv(sym, k0, count, p0, pairs, 0) + bias1
        value, rise = gelu_and_slope(pre)
        size = (count, pairs, PHASES, L)
        hid[pl.ds(k0, count), p0 : p0 + pairs] = value.astype(BF16).reshape(size)
        slope[pl.ds(k0, count), p0 : p0 + pairs] = rise.reshape(size)

    for box in inside:
        first_layer(*box)
    turn_wait_send(own, inbox1, relay1, 0)
    halo_wait(sym, 0)
    for box in around:
        first_layer(*box)
    clear_outside(hid)

    for q in range(NQ):
        k0 = q * QB
        pre = conv(hid, k0, QB, 0, nP, 1) + bias2
        value, rise = gelu_and_slope(pre)
        size = (QB, nP, PHASES, L)
        base = sym[pl.ds(k0 + 2, QB), 1 : nP + 1].astype(F32)
        fresh[pl.ds(k0, QB)] = (base + value.reshape(size)).astype(BF16)
        pull = cot[pl.ds(k0, QB)].astype(F32) * rise.reshape(size)
        g2[pl.ds(k0 + 2, QB), 1 : nP + 1] = pull.astype(BF16)
        halo_start(g2, 1, q)

    def first_pull(k0, count, p0, pairs):
        size = (count, pairs, PHASES, L)
        pulled = conv(g2, k0, count, p0, pairs, 2).reshape(size)
        rise = slope[pl.ds(k0, count), p0 : p0 + pairs]
        g1[pl.ds(k0, count), p0 : p0 + pairs] = (pulled * rise).astype(BF16)

    for box in inside:
        first_pull(*box)
    leave(fresh, out_ref)
    halo_wait(g2, 1)
    for box in around:
        first_pull(*box)

    clear_outside(g1)

    for q in range(NQ):
        k0 = q * QB
        total = conv(g1, k0, QB, 0, nP, 3).reshape(QB, nP, PHASES, L)
        gsym[pl.ds(k0, QB)] = (cot[pl.ds(k0, QB)].astype(F32) + total).astype(BF16)
        turn_start(gsym, inbox2, relay2, 1, [q])
    turn_relay(inbox2, relay2, 1)

    for q in range(NQ):
        turn_wait_recv(gsym, inbox2, 1, q)
        got = turned(inbox2, q, phase, lanes)
        for jp in range(nP):
            for b in range(2):
                i = q * QB + 2 * jp + b
                total = gsym[i].astype(F32) + got[:, jp, :, b * L : (b + 1) * L].astype(F32)
                fresh[i] = total.astype(BF16)
    turn_wait_send(gsym, inbox2, relay2, 1)
    leave(fresh, grad_ref)


def per_device(rows_axis, cols_axis, feature, w1, b1, w2, b2, cotangent):
    TR, TC, C = feature.shape
    nI, nP = TR // STEP, TC // (2 * STEP)
    QB, NQ, L = TC // STEP, TR // TC, 2 * C
    turned = lambda x: jnp.transpose(x, (1, 2, 0))
    image = lambda i, p: pltpu.VMEM((i, p, PHASES, L), BF16)
    vmem = pl.BlockSpec(memory_space=pltpu.VMEM)
    out = jax.ShapeDtypeStruct((TC, C, TR), BF16)
    res = pl.pallas_call(
        functools.partial(kernel, rows_axis, cols_axis),
        out_shape=(out, out),
        in_specs=[pl.BlockSpec(memory_space=pltpu.HBM)] * 6,
        out_specs=(vmem, vmem),
        scratch_shapes=[
            pltpu.VMEM((TC, C, TR), BF16),
            pltpu.VMEM(w1.shape, BF16),
            pltpu.VMEM((1, C), F32),
            pltpu.VMEM(w2.shape, BF16),
            pltpu.VMEM((1, C), F32),
            pltpu.VMEM((TC, C, TR), BF16),
            pltpu.SemaphoreType.DMA((6,)),
            pltpu.VMEM((nI * PHASES, STEP * TR), BF16),
            image(nI, nP),
            image(nI, nP),
            image(nI + 4, nP + 2),
            image(nI + 2, nP + 1),
            image(nI + 4, nP + 2),
            image(nI + 2, nP + 1),
            image(nI, nP),
            image(nI, nP),
            pltpu.VMEM((nI + 2, nP + 1, PHASES, L), F32),
            pltpu.VMEM((4, 12 * C, L), BF16),
            pltpu.VMEM((NQ, QB, nP, PHASES, L), BF16),
            pltpu.VMEM((NQ, QB, nP, PHASES, L), BF16),
            pltpu.VMEM((len(ROUTES), SLOTS, PARTS, QB // PARTS, nP, PHASES, L), BF16),
            pltpu.VMEM((len(ROUTES), SLOTS, PARTS, QB // PARTS, nP, PHASES, L), BF16),
            pltpu.SemaphoreType.DMA((2, 10)),
            pltpu.SemaphoreType.DMA((2, 10)),
            pltpu.SemaphoreType.DMA((2, NQ, PARTS)),
            pltpu.SemaphoreType.DMA((2, NQ, PARTS)),
            pltpu.SemaphoreType.DMA((2, len(ROUTES), SLOTS, PARTS)),
            pltpu.SemaphoreType.DMA((2, len(ROUTES), SLOTS, PARTS)),
        ],
        compiler_params=pltpu.CompilerParams(
            collective_id=0, has_side_effects=True, vmem_limit_bytes=30000000
        ),
    )(
        *(
            pltpu.with_memory_space_constraint(x, pltpu.HBM)
            for x in (
                turned(feature),
                w1,
                b1.reshape(1, C),
                w2,
                b2.reshape(1, C),
                turned(cotangent),
            )
        )
    )
    return tuple(jnp.transpose(x, (2, 0, 1)) for x in res)


def solution(mesh):
    specs = P("row", "col", None)
    return jax.shard_map(
        functools.partial(per_device, mesh.shape["row"], mesh.shape["col"]),
        mesh=mesh,
        in_specs=(specs, P(), P(), P(), P(), specs),
        out_specs=(specs, specs),
        check_vma=False,
    )
```
